256 devices in a mesh: tile: 64 (over z_hi, y, x, core), sub: 4 (over z_lo).
Axes of the slice: x: 4, y: 4, z: 8 (z_hi: 2, z_lo: 4; z = z_hi * 4 + z_lo), core: 2. Of those that a mesh axis runs over, the one named last changes fastest.
Arguments:
- pair_features: bfloat16 [64, 128, 128, 128], P('tile', 'sub'), may hold values from -6 to 6
- out_grad: bfloat16 [64, 128, 128, 128], P('tile', 'sub'), may hold values from -6 to 6
- bin_valid: int32 [2432], replicated, may hold values 0 or 1
- first_kernel: bfloat16 [3, 3, 128, 128], replicated, may hold values from -0.1875 to 0.1875
- first_bias: float32 [128], replicated, may hold values from -3 to 3
- second_kernel: bfloat16 [3, 3, 128, 128], replicated, may hold values from -0.1875 to 0.1875
- second_bias: float32 [128], replicated, may hold values from -3 to 3
Outputs:
- block_out: bfloat16 [64, 128, 128, 128], P('tile', 'sub')
- feature_grad: bfloat16 [64, 128, 128, 128], P('tile', 'sub')
- kernel_one_grad: float32 [3, 3, 128, 128], replicated
- bias_one_grad: float32 [128], replicated
- kernel_two_grad: float32 [3, 3, 128, 128], replicated
- bias_two_grad: float32 [128], replicated
The draws below stay inside these ranges and needn't reach their ends.
Inputs may be any that keep to these rules, and one draw needn't show every extreme that they name: `bin_valid`: 1 marks a bin that passed filtering.
All inputs are finite; a program needn't handle non-finite values.
Results may differ from the reference program's by a relative error of at most 0.006.
Values may be sent and summed in bfloat16 or wider, within the bound.
A program may use at most 128 MiB of HBM per device.

```python
import math
import jax
import jax.numpy as jnp
import numpy as np
from jax import lax

C = 128
TILE_BINS = 128
FIRST_DILATION = 8
SECOND_DILATION = 16
BAND_DIAGONALS = 4
TPG = 1
TILES = 64
TILE_ROWS = 16
COLS = 2432
N_TILE = 64


def set_ends(entries, own_key, low, high):
    place = [jax.random.randint(jax.random.fold_in(own_key, axis), (), 0, length) for axis, length in enumerate(entries.shape)]
    widest = entries.shape.index(max(entries.shape))
    next_to = place[:widest] + [(place[widest] + 1) % entries.shape[widest]] + place[widest + 1:]
    return entries.at[tuple(place)].set(low).at[tuple(next_to)].set(high)


def shard_levels(rng, extent, pieces, low, largest):
    def one(position, blocks):
        draws = jax.random.uniform(jax.random.fold_in(jax.random.fold_in(rng, 6), position), (blocks,), jnp.float32, low / len(pieces), largest / len(pieces))
        return jnp.repeat(jnp.exp(draws), extent[position] // blocks).reshape((-1,) + (1,) * (len(extent) - position - 1))

    level = one(*pieces[0])
    for cut in pieces[1:]:
        level = level * one(*cut)
    return level


def gaussian(key, shape, scale, most, split=(), held_as=jnp.bfloat16):
    result = jax.random.normal(key, shape, jnp.float32) * scale
    if len(split) > 0:
        result = shard_levels(key, shape, split, -0.22, 0.18) * result
    return jnp.clip(result, min=-most, max=most).astype(held_as)


def setup_inputs(seed: int = 0) -> dict:
    streams_of = jax.random.split(jax.random.key(seed), 8)
    pair_features = gaussian(streams_of[0], (TILES, TILE_BINS, TILE_BINS, C), 1.0, 6.0, ((0, 64), (1, 4)))
    out_grad = gaussian(streams_of[1], (TILES, TILE_BINS, TILE_BINS, C), 1.0, 6.0, ((0, 64), (1, 4)))
    bin_valid = set_ends((jax.random.randint(streams_of[2], (COLS,), 0, 10) < 9).astype(jnp.int32), jax.random.fold_in(streams_of[2], 1), 0, 1)
    first_kernel = gaussian(streams_of[3], (3, 3, C, C), (9 * C) ** -0.5, 0.1875)
    first_bias = gaussian(streams_of[4], (C,), 0.5, 3.0, (), jnp.float32)
    second_kernel = gaussian(streams_of[5], (3, 3, C, C), (9 * C) ** -0.5, 0.1875)
    second_bias = gaussian(streams_of[6], (C,), 0.5, 3.0, (), jnp.float32)
    return dict(pair_features=pair_features, out_grad=out_grad, bin_valid=bin_valid, first_kernel=first_kernel, first_bias=first_bias, second_kernel=second_kernel, second_bias=second_bias)


def tap_total_sum(sliding_window, kernel, dilation, anchor, out_rows, out_cols, flipped):
    channels = sliding_window.shape[-1]
    slot_count = sliding_window.shape[0]
    facing = -1 if flipped else 1
    running = jnp.zeros((slot_count * out_rows * out_cols, kernel.shape[-1]), jnp.float32)
    for row_tap in range(3):
        for col_tap in range(3):
            row_from = anchor + facing * (row_tap - 1) * dilation
            col_from = anchor + facing * (col_tap - 1) * dilation
            shifted = sliding_window[:, row_from:row_from + out_rows, col_from:col_from + out_cols, :].reshape(-1, channels)
            if flipped:
                running = running + lax.dot_general(shifted, kernel[row_tap, col_tap], (((1,), (1,)), ((), ())), preferred_element_type=jnp.float32)
            else:
                running = running + jnp.dot(shifted, kernel[row_tap, col_tap], preferred_element_type=jnp.float32)
    return running.reshape(slot_count, out_rows, out_cols, kernel.shape[-1])

def kernel_gradient(local_values, sliding_window, dilation, anchor):
    channels = local_values.shape[-1]
    out_rows = local_values.shape[1]
    out_cols = local_values.shape[2]
    flat_local = local_values.reshape(-1, channels)
    tap_grid = []
    for row_tap in range(3):
        tap_line = []
        for col_tap in range(3):
            row_from = anchor - (row_tap - 1) * dilation
            col_from = anchor - (col_tap - 1) * dilation
            shifted = sliding_window[:, row_from:row_from + out_rows, col_from:col_from + out_cols, :].reshape(-1, sliding_window.shape[-1])
            tap_line.append(lax.dot_general(flat_local, shifted, (((0,), (0,)), ((), ())), preferred_element_type=jnp.float32))
        tap_grid.append(jnp.stack(tap_line))
    return jnp.stack(tap_grid)

def neighbour_patch(band_array, band_tile_block, rim_width):
    tile_row = band_tile_block // BAND_DIAGONALS
    diagonal = band_tile_block % BAND_DIAGONALS
    row_blocks = []
    for row_step in (-1, 0, 1):
        col_blocks = []
        for col_step in (-1, 0, 1):
            other_row = tile_row + row_step
            other_diag = diagonal + col_step - row_step
            present = (other_row >= 0) & (other_row < TILE_ROWS) & (other_diag >= 0) & (other_diag < BAND_DIAGONALS)
            other_tile = jnp.clip(other_row * BAND_DIAGONALS + other_diag, 0, TILES - 1).astype(jnp.int32)
            neighbour = band_array[other_tile]
            col_blocks.append(jnp.where(present, neighbour, jnp.zeros((), band_array.dtype)))
        row_blocks.append(jnp.concatenate(col_blocks, axis=1))
    assembled = jnp.concatenate(row_blocks, axis=0)
    return assembled[TILE_BINS - rim_width:2 * TILE_BINS + rim_width, TILE_BINS - rim_width:2 * TILE_BINS + rim_width][None]

def reference(pair_features, out_grad, bin_valid, first_kernel, first_bias, second_kernel, second_bias):
    band_index = np.arange(TILES)
    linear_of_tile = (band_index - BAND_DIAGONALS) % TILES
    band_order = linear_of_tile % N_TILE * TPG + linear_of_tile // N_TILE
    position_order = (band_index % TPG * N_TILE + band_index // TPG + BAND_DIAGONALS) % TILES
    first_row = band_index // BAND_DIAGONALS * TILE_BINS
    first_col = (band_index // BAND_DIAGONALS + band_index % BAND_DIAGONALS) * TILE_BINS
    row_pos = jnp.asarray(first_row[:, None] + np.arange(TILE_BINS)[None, :], dtype=jnp.int32)
    col_pos = jnp.asarray(first_col[:, None] + np.arange(TILE_BINS)[None, :], dtype=jnp.int32)
    diagonal_distance = col_pos[:, None, :] - row_pos[:, :, None]
    valid_row_mask = bin_valid[row_pos] > 0
    valid_column_mask = bin_valid[col_pos] > 0
    live_cell_mask = ((diagonal_distance >= FIRST_DILATION + SECOND_DILATION) & (diagonal_distance <= (BAND_DIAGONALS - 1) * TILE_BINS - FIRST_DILATION - SECOND_DILATION) & valid_row_mask[:, :, None] & valid_column_mask[:, None, :]).astype(jnp.float32)
    live_wide = live_cell_mask[..., None]
    live_features = pair_features[band_order] * live_wide.astype(jnp.bfloat16)
    tile_ids = jnp.arange(TILES, dtype=jnp.int32)

    def first_conv(band_tile_block):
        sliding_window = neighbour_patch(live_features, band_tile_block, FIRST_DILATION)
        return tap_total_sum(sliding_window, first_kernel, FIRST_DILATION, FIRST_DILATION, TILE_BINS, TILE_BINS, False)[0] + first_bias
    pre_one = lax.map(first_conv, tile_ids)
    hidden_state = (jax.nn.silu(pre_one) * live_wide).astype(jnp.bfloat16)

    def second_conv(band_tile_block):
        sliding_window = neighbour_patch(hidden_state, band_tile_block, SECOND_DILATION)
        return tap_total_sum(sliding_window, second_kernel, SECOND_DILATION, SECOND_DILATION, TILE_BINS, TILE_BINS, False)[0] + second_bias
    pre_two = lax.map(second_conv, tile_ids)
    block_out = (live_features.astype(jnp.float32) + live_wide * pre_two).astype(jnp.bfloat16)
    second_gradient = out_grad[band_order] * live_wide.astype(jnp.bfloat16)

    def back_two(kernel_total_sum, band_tile_block):
        sliding_window = neighbour_patch(second_gradient, band_tile_block, SECOND_DILATION)
        kernel_total_sum = kernel_total_sum + kernel_gradient(hidden_state[band_tile_block][None], sliding_window, SECOND_DILATION, SECOND_DILATION)
        hidden_gradient = tap_total_sum(sliding_window, second_kernel, SECOND_DILATION, SECOND_DILATION, TILE_BINS, TILE_BINS, True)[0]
        pre_act = pre_one[band_tile_block]
        logistic = jax.nn.sigmoid(pre_act)
        silu_slope = logistic * (1.0 + pre_act * (1.0 - logistic))
        first_gradient = (hidden_gradient * live_wide[band_tile_block] * silu_slope).astype(jnp.bfloat16)
        return (kernel_total_sum, first_gradient)
    kernel_two_sum, first_gradient = lax.scan(back_two, jnp.zeros((3, 3, C, C), jnp.float32), tile_ids)
    ordered_grad = out_grad[band_order]

    def back_one(kernel_total_sum, band_tile_block):
        sliding_window = neighbour_patch(first_gradient, band_tile_block, FIRST_DILATION)
        kernel_total_sum = kernel_total_sum + kernel_gradient(live_features[band_tile_block][None], sliding_window, FIRST_DILATION, FIRST_DILATION)
        returned_values = tap_total_sum(sliding_window, first_kernel, FIRST_DILATION, FIRST_DILATION, TILE_BINS, TILE_BINS, True)[0]
        grad_tile = (live_wide[band_tile_block] * (ordered_grad[band_tile_block].astype(jnp.float32) + returned_values)).astype(jnp.bfloat16)
        return (kernel_total_sum, grad_tile)
    kernel_one_sum, feature_grad = lax.scan(back_one, jnp.zeros((3, 3, C, C), jnp.float32), tile_ids)
    grad_scale = 1.0 / math.sqrt(TILES * TILE_BINS * TILE_BINS)
    bias_one_grad = lax.optimization_barrier(jnp.sum(first_gradient.astype(jnp.float32), axis=(0, 1, 2))) * grad_scale
    bias_two_grad = lax.optimization_barrier(jnp.sum(second_gradient.astype(jnp.float32), axis=(0, 1, 2))) * grad_scale
    return (block_out[position_order], feature_grad[position_order], kernel_one_sum * grad_scale, bias_one_grad, kernel_two_sum * grad_scale, bias_two_grad)
```

```python
import functools
import math

import jax
import jax.numpy as jnp
from jax import lax
from jax.experimental import pallas as pl
from jax.experimental.pallas import tpu as pltpu
from jax.sharding import PartitionSpec as P

C = 128
D1 = 8
D2 = 16
DIAGS = 4
TILE_ROWS = 16
TILES = 64
ROWS = 32
SIDE = 128
VH = 24
HH = 32
PR = ROWS + 2 * VH
PC = SIDE + 2 * HH
HR, HC = ROWS + 2 * D2, SIDE + 2 * D2
GR, GC = ROWS + 2 * D1, SIDE + 2 * D1
LOW = D1 + D2
HIGH = (DIAGS - 1) * SIDE - D1 - D2
MESH = pl.DeviceIdType.MESH
F32 = jnp.float32
BF16 = jnp.bfloat16
PIECE = 80


def where_am_i():
    g = lax.axis_index("tile")
    s = lax.axis_index("sub")
    i = lax.rem(g + DIAGS, TILES) // DIAGS
    d = lax.rem(g, DIAGS)
    return g, s, i, d


def main_kernel(
    x_ref,
    g_ref,
    row_valid,
    col_valid,
    k1_ref,
    b1_ref,
    k2_ref,
    b2_ref,
    out_ref,
    fg_ref,
    acc1_ref,
    acc2_ref,
    bias_ref,
    xp,
    gp,
    xm,
    gm,
    hid,
    slope,
    gone,
    k1t,
    k2t,
    dist,
    send_sem,
    recv_sem,
    own_sem,
):
    g, s, i, d = where_am_i()
    up_g = jnp.where(s > 0, g, lax.rem(g + TILES - 3, TILES))
    up_s = jnp.where(s > 0, s - 1, 3)
    down_g = jnp.where(s < 3, g, lax.rem(g + 3, TILES))
    down_s = jnp.where(s < 3, s + 1, 0)
    left_g = lax.rem(g + TILES - 1, TILES)
    right_g = lax.rem(g + 1, TILES)
    has_up = (s > 0) | ((d <= 2) & (i > 0))
    has_down = (s < 3) | ((d >= 1) & (i < TILE_ROWS - 1))
    has_left = d > 0
    has_right = d < DIAGS - 1
    sides = {
        "up": (has_up, {"tile": up_g, "sub": up_s}),
        "down": (has_down, {"tile": down_g, "sub": down_s}),
        "left": (has_left, {"tile": left_g, "sub": s}),
        "right": (has_right, {"tile": right_g, "sub": s}),
    }

    own = []
    for n, (src, dst) in enumerate(((x_ref, xp), (g_ref, gp))):
        cp = pltpu.make_async_copy(
            src, dst.at[pl.ds(VH, ROWS), pl.ds(HH, SIDE)], own_sem.at[n]
        )
        cp.start()
        own.append(cp)

    barrier = pltpu.get_barrier_semaphore()
    for has, dev in sides.values():

        @pl.when(has)
        def _():
            pl.semaphore_signal(barrier, inc=1, device_id=dev, device_id_type=MESH)

    count = sum(has.astype(jnp.int32) for has, _ in sides.values())
    pl.semaphore_wait(barrier, count)

    def plan(src, win):
        moves = {}
        for name, c, n in (("l", 0, HH), ("r", SIDE - HH, HH), ("m", HH, SIDE - 2 * HH)):
            moves["down_" + name] = (
                "down",
                src.at[pl.ds(ROWS - VH, VH), pl.ds(c, n)],
                win.at[pl.ds(0, VH), pl.ds(HH + c, n)],
            )
            moves["up_" + name] = (
                "up",
                src.at[pl.ds(0, VH), pl.ds(c, n)],
                win.at[pl.ds(VH + ROWS, VH), pl.ds(HH + c, n)],
            )
        moves["left"] = (
            "left",
            src.at[pl.ds(0, ROWS), pl.ds(0, HH)],
            win.at[pl.ds(VH, ROWS), pl.ds(HH + SIDE, HH)],
        )
        moves["right"] = (
            "right",
            src.at[pl.ds(0, ROWS), pl.ds(SIDE - HH, HH)],
            win.at[pl.ds(VH, ROWS), pl.ds(0, HH)],
        )
        for name, r in (("top", 0), ("bottom", VH + ROWS)):
            moves["left_" + name] = (
                "left",
                win.at[pl.ds(r, VH), pl.ds(HH, HH)],
                win.at[pl.ds(r, VH), pl.ds(HH + SIDE, HH)],
            )
            moves["right_" + name] = (
                "right",
                win.at[pl.ds(r, VH), pl.ds(SIDE, HH)],
                win.at[pl.ds(r, VH), pl.ds(0, HH)],
            )
        return moves

    opposite = {"up": "down", "down": "up", "left": "right", "right": "left"}
    plans = (plan(x_ref, xp), plan(g_ref, gp))
    names = list(plans[0])

    def copy_of(a, name):
        way, src, dst = plans[a][name]
        n = a * len(names) + names.index(name)
        return pltpu.make_async_remote_copy(
            src_ref=src,
            dst_ref=dst,
            send_sem=send_sem.at[n],
            recv_sem=recv_sem.at[n],
            device_id=sides[way][1],
            device_id_type=MESH,
        )

    def start(a, name):
        @pl.when(sides[plans[a][name][0]][0])
        def _():
            copy_of(a, name).start()

    def sent(a, name):
        @pl.when(sides[plans[a][name][0]][0])
        def _():
            copy_of(a, name).wait_send()

    def arrived(a, name):
        @pl.when(sides[opposite[plans[a][name][0]]][0])
        def _():
            copy_of(a, name).wait_recv()

    first = ("down_l", "up_l", "down_r", "up_r", "left", "right", "down_m", "up_m")
    relays = {
        "left_top": "down_l",
        "right_top": "down_r",
        "left_bottom": "up_l",
        "right_bottom": "up_r",
    }
    for a in range(2):
        for name in first:
            start(a, name)

    def relay(a):
        for name in ("down_l", "up_l", "down_r", "up_r"):
            arrived(a, name)
        for name in relays:
            start(a, name)

    for t in range(9):
        u, w = divmod(t, 3)
        k1t[pl.ds((8 - t) * C, C), :] = k1_ref[t].T
        k2t[pl.ds((8 - t) * C, C), :] = k2_ref[t].T
    a0 = i * SIDE + s * ROWS - VH
    b0 = (i + d) * SIDE - HH
    cols = lax.broadcasted_iota(jnp.int32, (PC, C), 0) + (b0 - a0)
    dist[...] = jnp.where(col_valid[...] > 0, cols, -100000)

    def mask(r, c, n):
        far = jnp.where(row_valid[r] > 0, 0, 1000000)
        here = dist[pl.ds(c, n), :]
        return (here >= LOW + r + far) & (here <= HIGH + r)

    def mask_rows(src, dst, r):
        v = src[r].astype(F32)
        dst[r] = jnp.where(mask(r, 0, PC), v, 0.0).astype(BF16)

    def taps(ref, r, n, c, m, dil):
        parts = []
        for u in (-1, 0, 1):
            for w in (-1, 0, 1):
                v = ref[pl.ds(r + u * dil, n), c + w * dil : c + w * dil + m, :]
                parts.append(v.reshape(n * m, C))
        return jnp.concatenate(parts, axis=1)

    def conv(ref, r, n, c, m, dil, kernel):
        return jnp.dot(taps(ref, r, n, c, m, dil), kernel, preferred_element_type=F32)

    relay(0)
    own[0].wait()
    for name in ("left", "right", "down_m", "up_m") + tuple(relays):
        arrived(0, name)

    @pl.loop(0, PR)
    def _(r):
        mask_rows(xp, xm, r)

    bias1 = jnp.broadcast_to(b1_ref[...], (HC, C))
    k1 = k1_ref[...].reshape(9 * C, C)

    def hidden_rows(r, n):
        pre = conv(xm, r + D1, n, HH - D2, HC, D1, k1).reshape(n, HC, C)
        for q in range(n):
            v = pre[q] + bias1
            sig = 1.0 / (1.0 + jnp.exp(-v))
            live = mask(r + q + D1, HH - D2, HC)
            hid[r + q] = jnp.where(live, v * sig, 0.0).astype(BF16)
            sl = jnp.where(live, sig * (1.0 + v * (1.0 - sig)), 0.0)
            slope[r + q] = sl[D1 : D1 + GC]

    @pl.loop(0, HR // 2)
    def _(q):
        hidden_rows(q * 2, 2)

    relay(1)
    own[1].wait()
    for name in ("left", "right", "down_m", "up_m") + tuple(relays):
        arrived(1, name)

    @pl.loop(0, PR)
    def _(r):
        mask_rows(gp, gm, r)

    bias2 = jnp.broadcast_to(b2_ref[...], (SIDE, C))
    k2 = k2_ref[...].reshape(9 * C, C)

    @pl.loop(0, ROWS // 2)
    def _(q):
        r = q * 2
        pre = conv(hid, r + D2, 2, D2, SIDE, D2, k2).reshape(2, SIDE, C)
        for e in range(2):
            live = mask(r + e + VH, HH, SIDE)
            x = xm[r + e + VH, HH : HH + SIDE, :].astype(F32)
            out_ref[r + e] = (x + jnp.where(live, pre[e] + bias2, 0.0)).astype(BF16)

    @pl.loop(0, GR // 2)
    def _(q):
        r = q * 2
        hg = conv(gm, r + VH - D1, 2, HH - D1, GC, D2, k2t[...]).reshape(2, GC, C)
        for e in range(2):
            gone[r + e] = (hg[e] * slope[r + e + D1]).astype(BF16)

    @pl.loop(0, ROWS // 2)
    def _(q):
        r = q * 2
        back = conv(gone, r + D1, 2, D1, SIDE, D1, k1t[...]).reshape(2, SIDE, C)
        for e in range(2):
            live = mask(r + e + VH, HH, SIDE)
            o = gm[r + e + VH, HH : HH + SIDE, :].astype(F32)
            fg_ref[r + e] = (o + jnp.where(live, back[e], 0.0)).astype(BF16)

    acc1_ref[...] = jnp.zeros_like(acc1_ref)
    acc2_ref[...] = jnp.zeros_like(acc2_ref)
    bias_ref[...] = jnp.zeros_like(bias_ref)
    step = 8

    def folded(v):
        v = v.astype(F32).reshape(step * SIDE // 8, 8, C)
        return jnp.sum(v, axis=0)

    @pl.loop(0, ROWS // step)
    def _(q):
        r = q * step
        gv = gm[pl.ds(r + VH, step), HH : HH + SIDE, :].reshape(step * SIDE, C)
        hv = taps(hid, r + D2, step, D2, SIDE, D2)
        acc2_ref[...] += lax.dot_general(
            gv, hv, (((0,), (0,)), ((), ())), preferred_element_type=F32
        )
        dv = gone[pl.ds(r + D1, step), D1 : D1 + SIDE, :].reshape(step * SIDE, C)
        xv = taps(xm, r + VH, step, HH, SIDE, D1)
        acc1_ref[...] += lax.dot_general(
            dv, xv, (((0,), (0,)), ((), ())), preferred_element_type=F32
        )
        bias_ref[0] += folded(dv)
        bias_ref[1] += folded(gv)

    for a in range(2):
        for name in names:
            sent(a, name)


def main_call(x, gr, row_valid, col_valid, k1, b1, k2, b2):
    vmem = pl.BlockSpec(memory_space=pltpu.VMEM)
    n = 2 * 12
    return pl.pallas_call(
        main_kernel,
        out_shape=(
            jax.ShapeDtypeStruct((ROWS, SIDE, C), BF16),
            jax.ShapeDtypeStruct((ROWS, SIDE, C), BF16),
            jax.ShapeDtypeStruct((C, 9 * C), F32),
            jax.ShapeDtypeStruct((C, 9 * C), F32),
            jax.ShapeDtypeStruct((2, 8, C), F32),
        ),
        in_specs=[
            pl.BlockSpec(memory_space=pl.ANY),
            pl.BlockSpec(memory_space=pl.ANY),
            pl.BlockSpec(memory_space=pltpu.SMEM),
            vmem,
            vmem,
            vmem,
            vmem,
            vmem,
        ],
        out_specs=(vmem,) * 5,
        scratch_shapes=[
            pltpu.VMEM((PR, PC, C), BF16),
            pltpu.VMEM((PR, PC, C), BF16),
            pltpu.VMEM((PR, PC, C), BF16),
            pltpu.VMEM((PR, PC, C), BF16),
            pltpu.VMEM((HR, HC, C), BF16),
            pltpu.VMEM((HR, GC, C), F32),
            pltpu.VMEM((GR, GC, C), BF16),
            pltpu.VMEM((9 * C, C), BF16),
            pltpu.VMEM((9 * C, C), BF16),
            pltpu.VMEM((PC, C), jnp.int32),
            pltpu.SemaphoreType.DMA((n,)),
            pltpu.SemaphoreType.DMA((n,)),
            pltpu.SemaphoreType.DMA((2,)),
        ],
        compiler_params=pltpu.CompilerParams(
            collective_id=0, has_side_effects=True, vmem_limit_bytes=60 * 1024 * 1024
        ),
        name="resblock",
    )(x, gr, row_valid, col_valid, k1, b1, k2, b2)


def reduce_kernel(
    a1_ref, a2_ref, bias_ref, out_ref, s1, r1, t1, s2, r2, s3, r3, send_sem, recv_sem
):
    g, s, _, _ = where_am_i()
    xc = lax.rem(g, 8)
    y = lax.rem(g // 8, 4)
    z = (g // 32) * 4 + s

    def xc_peer(j):
        return {"tile": g - xc + lax.rem(xc + j, 8), "sub": s}

    def y_peer(j):
        return {"tile": g - 8 * y + 8 * lax.rem(y + j, 4), "sub": s}

    def z_peer(j):
        other = lax.rem(z + j, 8)
        return {"tile": lax.rem(g, 32) + 32 * (other // 4), "sub": lax.rem(other, 4)}

    peers = (
        [xc_peer(j) for j in range(1, 8)]
        + [y_peer(j) for j in range(1, 4)]
        + [z_peer(j) for j in range(1, 8)]
    )
    barrier = pltpu.get_barrier_semaphore()
    for dev in peers:
        pl.semaphore_signal(barrier, inc=1, device_id=dev, device_id_type=MESH)

    def rows_of(p):
        return (p // 4, p % 4)

    per = PIECE * 32
    flat = s1

    def put(row, v):
        a, b, r = row // (4 * PIECE), row // PIECE % 4, row % PIECE
        flat[a, b, pl.ds(r, v.shape[0]), :] = v.astype(BF16)

    for n, ref in enumerate((a1_ref, a2_ref)):
        for t in range(9):
            for q in range(8):
                row = n * 9 * C + t * C + q * 16
                put(row, ref[pl.ds(q * 16, 16), t * C : (t + 1) * C])
    put(18 * C, bias_ref[...].reshape(16, C))
    for row in range(18 * C + 16, per, 16):
        put(row, jnp.zeros((16, C), F32))

    pl.semaphore_wait(barrier, len(peers))

    def remote(src, dst, n, dev):
        return pltpu.make_async_remote_copy(
            src_ref=src,
            dst_ref=dst,
            send_sem=send_sem.at[n],
            recv_sem=recv_sem.at[n],
            device_id=dev,
            device_id_type=MESH,
        )

    copies = []
    for j in range(1, 8):
        cp = remote(s1.at[lax.rem(xc + j, 8)], r1.at[j - 1], j - 1, xc_peer(j))
        cp.start()
        copies.append(cp)
    t1[...] = s1[xc].astype(F32)
    for j in range(1, 8):
        copies[j - 1].wait_recv()
        t1[...] += r1[j - 1].astype(F32)
    s2[...] = t1[...].astype(BF16)
    for j in range(1, 4):
        cp = remote(s2.at[lax.rem(y + j, 4)], r2.at[j - 1], 6 + j, y_peer(j))
        cp.start()
        copies.append(cp)
    total = t1[y]
    for j in range(1, 4):
        copies[6 + j].wait_recv()
        total = total + r2[j - 1].astype(F32)
    s3[...] = total.astype(BF16)
    for j in range(1, 8):
        cp = remote(s3, r3.at[z], 9 + j, z_peer(j))
        cp.start()
        copies.append(cp)
    r3[z] = s3[...]
    for j in range(1, 8):
        copies[9 + j].wait_recv()
    total = r3[0].astype(F32)
    for j in range(1, 8):
        total = total + r3[j].astype(F32)
    out_ref[xc, y] = total.astype(BF16)
    for j in range(1, 4):
        cp = remote(out_ref.at[xc, y], out_ref.at[xc, y], 16 + j, y_peer(j))
        cp.start()
        copies.append(cp)
    for j in range(1, 4):
        copies[16 + j].wait_recv()
    for j in range(1, 8):
        cp = remote(out_ref.at[xc], out_ref.at[xc], 19 + j, xc_peer(j))
        cp.start()
        copies.append(cp)
    for j in range(1, 8):
        copies[19 + j].wait_recv()
    for cp in copies:
        cp.wait_send()


def reduce_call(a1, a2, bias):
    vmem = pl.BlockSpec(memory_space=pltpu.VMEM)
    return pl.pallas_call(
        reduce_kernel,
        out_shape=jax.ShapeDtypeStruct((8, 4, PIECE, C), BF16),
        in_specs=[vmem] * 3,
        out_specs=vmem,
        scratch_shapes=[
            pltpu.VMEM((8, 4, PIECE, C), BF16),
            pltpu.VMEM((7, 4, PIECE, C), BF16),
            pltpu.VMEM((4, PIECE, C), F32),
            pltpu.VMEM((4, PIECE, C), BF16),
            pltpu.VMEM((3, PIECE, C), BF16),
            pltpu.VMEM((PIECE, C), BF16),
            pltpu.VMEM((8, PIECE, C), BF16),
            pltpu.SemaphoreType.DMA((27,)),
            pltpu.SemaphoreType.DMA((27,)),
        ],
        compiler_params=pltpu.CompilerParams(collective_id=1, has_side_effects=True),
        name="reduce",
    )(a1, a2, bias)


def on_device(x, gr, bin_valid, k1, b1, k2, b2):
    g, s, i, d = where_am_i()
    map_rows = TILE_ROWS * SIDE
    rows = jnp.pad(bin_valid[:map_rows], (VH, VH))
    cols = jnp.pad(bin_valid, (HH, HH))
    row_valid = lax.dynamic_slice_in_dim(rows, i * SIDE + s * ROWS, PR)
    col_valid = lax.dynamic_slice_in_dim(cols, (i + d) * SIDE, PC)
    col_valid = jnp.broadcast_to(col_valid[:, None], (PC, C))
    block_out, feature_grad, acc1, acc2, bias = main_call(
        x[0],
        gr[0],
        row_valid,
        col_valid,
        k1.reshape(9, C, C),
        b1[None],
        k2.reshape(9, C, C),
        b2[None],
    )
    total = reduce_call(acc1, acc2, bias).reshape(32 * PIECE, C).astype(F32)
    total = total * (1.0 / math.sqrt(TILES * SIDE * SIDE))
    grads = total[: 18 * C].reshape(2, 3, 3, C, C).swapaxes(-1, -2)
    bias = jnp.sum(total[18 * C : 18 * C + 16].reshape(2, 8, C), axis=1)
    return block_out[None], feature_grad[None], grads[0], bias[0], grads[1], bias[1]


def solution(mesh):
    strip = P("tile", "sub", None, None)
    return jax.shard_map(
        on_device,
        mesh=mesh,
        in_specs=(strip, strip, P(), P(), P(), P(), P()),
        out_specs=(strip, strip, P(), P(), P(), P()),
        check_vma=False,
    )
```

```python
import math

import jax
import jax.numpy as jnp
from jax import lax
from jax.experimental import pallas as pl
from jax.experimental.pallas import tpu as pltpu
from jax.sharding import PartitionSpec as P

C = 128
D1 = 8
D2 = 16
DIAGS = 4
TILE_ROWS = 16
TILES = 64
ROWS = 32
SIDE = 128
VH = 24
HH = 32
PR = ROWS + 2 * VH
PC = SIDE + 2 * HH
HR, HC = ROWS + 2 * D2, SIDE + 2 * D2
GR, GC = ROWS + 2 * D1, SIDE + 2 * D1
LOW = D1 + D2
HIGH = (DIAGS - 1) * SIDE - D1 - D2
MESH = pl.DeviceIdType.MESH
F32 = jnp.float32
BF16 = jnp.bfloat16
PIECE = 40
KR = 9 * C
SCALE = 1.0 / math.sqrt(TILES * SIDE * SIDE)
HALO = 14
COPIES = 27


def where_am_i():
    g = lax.axis_index("tile")
    s = lax.axis_index("sub")
    i = lax.rem(g + DIAGS, TILES) // DIAGS
    d = lax.rem(g, DIAGS)
    return g, s, i, d


class Reduction:
    def __init__(self, g, s, bufs, send_sem, recv_sem, first):
        self.s1, self.r1, self.t1, self.s2, self.r2, self.s3, self.r3, self.all = bufs
        self.xc = lax.rem(g, 8)
        self.y = lax.rem(g // 8, 4)
        self.z = (g // 32) * 4 + s
        self.g, self.s = g, s
        self.sems = (send_sem, recv_sem)
        self.first = first
        self.copies = []

    def xc_peer(self, j):
        return {"tile": self.g - self.xc + lax.rem(self.xc + j, 8), "sub": self.s}

    def y_peer(self, j):
        return {"tile": self.g - 8 * self.y + 8 * lax.rem(self.y + j, 4), "sub": self.s}

    def z_peer(self, j):
        other = lax.rem(self.z + j, 8)
        return {"tile": lax.rem(self.g, 32) + 32 * (other // 4), "sub": lax.rem(other, 4)}

    def peers(self):
        return (
            [self.xc_peer(j) for j in range(1, 8)]
            + [self.y_peer(j) for j in range(1, 4)]
            + [self.z_peer(j) for j in range(1, 8)]
        )

    def send(self, src, dst, dev):
        n = self.first + len(self.copies)
        cp = pltpu.make_async_remote_copy(
            src_ref=src,
            dst_ref=dst,
            send_sem=self.sems[0].at[n],
            recv_sem=self.sems[1].at[n],
            device_id=dev,
            device_id_type=MESH,
        )
        cp.start()
        self.copies.append(cp)

    def put(self, row, v):
        v = v.astype(BF16)
        for q in range(0, v.shape[0], 8):
            p, r = divmod(row + q, PIECE)
            self.s1[p // 4, p % 4, r : r + 8, :] = v[q : q + 8]

    def load(self, acc, bias):
        for t in range(9):
            self.put(t * C, acc[:, t * C : (t + 1) * C].T)
        self.put(KR, bias[...])
        self.put(KR + 8, jnp.zeros((32 * PIECE - KR - 8, C), F32))

    def start(self):
        for j in range(1, 8):
            self.send(self.s1.at[lax.rem(self.xc + j, 8)], self.r1.at[j - 1], self.xc_peer(j))

    def over_y(self):
        for j in range(7):
            self.copies[j].wait_recv()
        total = self.s1[self.xc].astype(F32)
        for j in range(7):
            total = total + self.r1[j].astype(F32)
        self.t1[...] = total
        self.s2[...] = total.astype(BF16)
        for j in range(1, 4):
            self.send(self.s2.at[lax.rem(self.y + j, 4)], self.r2.at[j - 1], self.y_peer(j))

    def over_z(self):
        for j in range(3):
            self.copies[7 + j].wait_recv()
        total = self.t1[self.y]
        for j in range(3):
            total = total + self.r2[j].astype(F32)
        self.s3[...] = total.astype(BF16)
        for j in range(1, 8):
            self.send(self.s3, self.r3.at[self.z], self.z_peer(j))
        self.r3[self.z] = self.s3[...]

    def back_y(self):
        for j in range(7):
            self.copies[10 + j].wait_recv()
        total = self.r3[0].astype(F32)
        for j in range(1, 8):
            total = total + self.r3[j].astype(F32)
        self.all[self.xc, self.y] = total.astype(BF16)
        own = self.all.at[self.xc, self.y]
        for j in range(1, 4):
            self.send(own, own, self.y_peer(j))

    def back_xc(self):
        for j in range(3):
            self.copies[17 + j].wait_recv()
        own = self.all.at[self.xc]
        for j in range(1, 8):
            self.send(own, own, self.xc_peer(j))

    def finish(self, kernel_ref, bias_ref):
        for j in range(7):
            self.copies[20 + j].wait_recv()
        for p in range(KR // PIECE + 1):
            n = min(PIECE, KR - p * PIECE)
            kernel_ref[p * PIECE : p * PIECE + n, :] = (
                self.all[p // 4, p % 4, 0:n, :].astype(F32) * SCALE
            )
        p, r = divmod(KR, PIECE)
        tail = self.all[p // 4, p % 4].astype(F32)[r : r + 8]
        bias_ref[...] = jnp.sum(tail, axis=0, keepdims=True) * SCALE
        for cp in self.copies:
            cp.wait_send()


def main_kernel(
    x_ref,
    g_ref,
    valid_ref,
    k1_ref,
    b1_ref,
    k2_ref,
    b2_ref,
    out_ref,
    fg_ref,
    kg1_ref,
    bg1_ref,
    kg2_ref,
    bg2_ref,
    xp,
    gp,
    xm,
    gm,
    hid,
    slope,
    gone,
    k1t,
    k2t,
    w1,
    w1t,
    w2,
    w2t,
    dist,
    acc,
    bias,
    s1,
    r1,
    t1,
    s2,
    r2,
    s3,
    r3,
    everything,
    send_sem,
    recv_sem,
    own_sem,
    red_send,
    red_recv,
):
    g, s, i, d = where_am_i()
    bufs = (s1, r1, t1, s2, r2, s3, r3, everything)
    red1, red2 = (
        Reduction(g, s, [b.at[n] for b in bufs], red_send, red_recv, n * COPIES) for n in range(2)
    )
    up_g = jnp.where(s > 0, g, lax.rem(g + TILES - 3, TILES))
    up_s = jnp.where(s > 0, s - 1, 3)
    down_g = jnp.where(s < 3, g, lax.rem(g + 3, TILES))
    down_s = jnp.where(s < 3, s + 1, 0)
    left_g = lax.rem(g + TILES - 1, TILES)
    right_g = lax.rem(g + 1, TILES)
    has_up = (s > 0) | ((d <= 2) & (i > 0))
    has_down = (s < 3) | ((d >= 1) & (i < TILE_ROWS - 1))
    has_left = d > 0
    has_right = d < DIAGS - 1
    sides = {
        "up": (has_up, {"tile": up_g, "sub": up_s}),
        "down": (has_down, {"tile": down_g, "sub": down_s}),
        "left": (has_left, {"tile": left_g, "sub": s}),
        "right": (has_right, {"tile": right_g, "sub": s}),
    }

    own = []
    for n, (src, dst) in enumerate(((x_ref, xp), (g_ref, gp))):
        cp = pltpu.make_async_copy(
            src, dst.at[pl.ds(VH, ROWS), pl.ds(HH, SIDE)], own_sem.at[n]
        )
        cp.start()
        own.append(cp)

    barrier = pltpu.get_barrier_semaphore()
    for has, dev in sides.values():

        @pl.when(has)
        def _():
            pl.semaphore_signal(barrier, inc=1, device_id=dev, device_id_type=MESH)

    for dev in red1.peers():
        pl.semaphore_signal(barrier, inc=1, device_id=dev, device_id_type=MESH)
    count = sum(has.astype(jnp.int32) for has, _ in sides.values())
    pl.semaphore_wait(barrier, count + 17)

    def live_piece(way, p, diag, sub):
        if way == "up":
            return ((diag != 0) | (p >= sub)) & ((diag != DIAGS - 1) | (p < sub))
        return ((diag != 0) | (p > sub)) & ((diag != DIAGS - 1) | (p <= sub))

    above_d, above_s = jnp.where(s > 0, d, d + 1), jnp.where(s > 0, s - 1, 3)
    below_d, below_s = jnp.where(s < 3, d, d - 1), jnp.where(s < 3, s + 1, 0)

    def plan(src, win):
        moves = {}
        for p in range(4):
            c = p * HH
            moves[f"down_{p}"] = (
                has_down & live_piece("down", p, d, s),
                has_up & live_piece("down", p, above_d, above_s),
                sides["down"][1],
                src.at[pl.ds(ROWS - VH, VH), pl.ds(c, HH)],
                win.at[pl.ds(0, VH), pl.ds(HH + c, HH)],
            )
            moves[f"up_{p}"] = (
                has_up & live_piece("up", p, d, s),
                has_down & live_piece("up", p, below_d, below_s),
                sides["up"][1],
                src.at[pl.ds(0, VH), pl.ds(c, HH)],
                win.at[pl.ds(VH + ROWS, VH), pl.ds(HH + c, HH)],
            )
        moves["left"] = (
            has_left,
            has_right,
            sides["left"][1],
            src.at[pl.ds(0, ROWS), pl.ds(0, HH)],
            win.at[pl.ds(VH, ROWS), pl.ds(HH + SIDE, HH)],
        )
        moves["right"] = (
            has_right,
            has_left,
            sides["right"][1],
            src.at[pl.ds(0, ROWS), pl.ds(SIDE - HH, HH)],
            win.at[pl.ds(VH, ROWS), pl.ds(0, HH)],
        )
        for name, r in (("top", 0), ("bottom", VH + ROWS)):
            moves["left_" + name] = (
                has_left,
                has_right,
                sides["left"][1],
                win.at[pl.ds(r, VH), pl.ds(HH, HH)],
                win.at[pl.ds(r, VH), pl.ds(HH + SIDE, HH)],
            )
            moves["right_" + name] = (
                has_right,
                has_left,
                sides["right"][1],
                win.at[pl.ds(r, VH), pl.ds(SIDE, HH)],
                win.at[pl.ds(r, VH), pl.ds(0, HH)],
            )
        return moves

    plans = (plan(x_ref, xp), plan(g_ref, gp))
    names = list(plans[0])

    def copy_of(a, name):
        _, _, dev, src, dst = plans[a][name]
        n = a * HALO + names.index(name)
        return pltpu.make_async_remote_copy(
            src_ref=src,
            dst_ref=dst,
            send_sem=send_sem.at[n],
            recv_sem=recv_sem.at[n],
            device_id=dev,
            device_id_type=MESH,
        )

    def start(a, name):
        @pl.when(plans[a][name][0])
        def _():
            copy_of(a, name).start()

    def sent(a, name):
        @pl.when(plans[a][name][0])
        def _():
            copy_of(a, name).wait_send()

    def arrived(a, name):
        @pl.when(plans[a][name][1])
        def _():
            copy_of(a, name).wait_recv()

    edges = ("down_0", "up_0", "down_3", "up_3")
    middles = ("down_1", "up_1", "down_2", "up_2")
    relays = ("left_top", "right_top", "left_bottom", "right_bottom")
    for a in range(2):
        for name in edges + ("left", "right") + middles:
            start(a, name)

    def relay(a):
        for name in edges:
            arrived(a, name)
        for name in relays:
            start(a, name)

    for t in range(9):
        k1t[pl.ds((8 - t) * C, C), :] = k1_ref[t].T
        k2t[pl.ds((8 - t) * C, C), :] = k2_ref[t].T
    zero = jnp.zeros((3 * C, C), BF16)
    k1, k2 = k1_ref[...].reshape(9 * C, C), k2_ref[...].reshape(9 * C, C)
    for dst, src in ((w1, k1), (w2, k2), (w1t, k1t[...]), (w2t, k2t[...])):
        dst[0 : 9 * C, 0:C] = src
        dst[9 * C : 12 * C, 0:C] = zero
        dst[0 : 3 * C, C : 2 * C] = zero
        dst[3 * C : 12 * C, C : 2 * C] = src
    a0 = i * SIDE + s * ROWS - VH
    b0 = (i + d) * SIDE - HH
    n_bins = valid_ref.shape[0]

    @pl.loop(0, PC)
    def _(c):
        b = b0 + c
        ok = (b >= 0) & (b < n_bins) & (valid_ref[jnp.clip(b, 0, n_bins - 1)] > 0)
        dist[pl.ds(c, 1), :] = jnp.full((1, C), jnp.where(ok, b - a0, -100000), jnp.int32)

    def mask(r, c, n):
        a = a0 + r
        last = TILE_ROWS * SIDE - 1
        ok = (a >= 0) & (a <= last) & (valid_ref[jnp.clip(a, 0, last)] > 0)
        far = jnp.where(ok, 0, 1000000)
        here = dist[c : c + n, :]
        return (here >= LOW + r + far) & (here <= HIGH + r)

    def masked(src, r, c, n):
        return jnp.where(mask(r, c, n), src[r, c : c + n, :].astype(F32), 0.0).astype(BF16)

    def gather(ref, r, n, c, m, dil, us):
        parts = []
        for u in us:
            for w in (-1, 0, 1):
                v = ref[pl.ds(r + u * dil, n), c + w * dil : c + w * dil + m, :]
                parts.append(v.reshape(n * m, C))
        return jnp.concatenate(parts, axis=1)

    def taps(ref, r, n, c, m, dil):
        return gather(ref, r, n, c, m, dil, (-1, 0, 1))

    def pair(ref, r, n, c, m, dil, kernel):
        v = gather(ref, r, n, c, m, dil, (-1, 0, 1, 2))
        both = jnp.dot(v, kernel[...], preferred_element_type=F32)
        return both[:, :C].reshape(n, m, C), both[:, C:].reshape(n, m, C)

    def rows_of(both, dil):
        return [(h * dil + k, both[h][k]) for h in range(2) for k in range(both[h].shape[0])]

    N = 8

    relay(0)
    own[0].wait()
    for name in ("left", "right") + middles + relays:
        arrived(0, name)

    @pl.loop(0, PR)
    def _(r):
        xm[r] = masked(xp, r, 0, PC)

    bias1 = jnp.broadcast_to(b1_ref[...], (HC, C))

    @pl.loop(0, HR // 16)
    def _(q):
        r = q * 16
        for e, pre in rows_of(pair(xm, r + D1, N, HH - D2, HC, D1, w1), D1):
            v = pre + bias1
            sig = 1.0 / (1.0 + jnp.exp(-v))
            live = mask(r + e + D1, HH - D2, HC)
            hid[r + e] = jnp.where(live, v * sig, 0.0).astype(BF16)
            sl = jnp.where(live, sig * (1.0 + v * (1.0 - sig)), 0.0)
            slope[r + e] = sl[D1 : D1 + GC]

    own[1].wait()

    @pl.loop(0, ROWS)
    def _(r):
        gm[r + VH, HH : HH + SIDE, :] = masked(gp, r + VH, HH, SIDE)

    step = 8

    def kernel_gradient(cots, row, col, values, vrow, vcol, dil):
        acc[...] = jnp.zeros_like(acc)
        bias[...] = jnp.zeros_like(bias)

        @pl.loop(0, ROWS // step)
        def _(q):
            r = q * step
            cv = cots[pl.ds(r + row, step), col : col + SIDE, :].reshape(step * SIDE, C)
            vv = taps(values, r + vrow, step, vcol, SIDE, dil)
            acc[...] += lax.dot_general(
                cv, vv, (((0,), (0,)), ((), ())), preferred_element_type=F32
            )
            folded = cv.astype(F32).reshape(step * SIDE // 8, 8, C)
            bias[...] += jnp.sum(folded, axis=0)

    kernel_gradient(gm, VH, HH, hid, D2, D2, D2)
    red2.load(acc, bias)
    red2.start()

    bias2 = jnp.broadcast_to(b2_ref[...], (SIDE, C))

    @pl.loop(0, D2 // N)
    def _(q):
        r = q * N
        for e, pre in rows_of(pair(hid, r + D2, N, D2, SIDE, D2, w2), D2):
            live = mask(r + e + VH, HH, SIDE)
            x = xm[r + e + VH, HH : HH + SIDE, :].astype(F32)
            out_ref[r + e] = (x + jnp.where(live, pre + bias2, 0.0)).astype(BF16)

    relay(1)
    red2.over_y()
    red2.over_z()
    for name in ("left", "right") + middles + relays:
        arrived(1, name)

    @pl.loop(0, PR)
    def _(r):
        gm[r] = masked(gp, r, 0, PC)

    @pl.loop(0, D2 // N)
    def _(q):
        r = q * N
        for e, hg in rows_of(pair(gm, r + VH - D1, N, HH - D1, GC, D2, w2t), D2):
            gone[r + e] = (hg * slope[r + e + D1]).astype(BF16)

    @pl.loop(0, D2 // N)
    def _(q):
        r = q * N + 2 * D2
        v = taps(gm, r + VH - D1, N, HH - D1, GC, D2)
        hg = jnp.dot(v, k2t[...], preferred_element_type=F32).reshape(N, GC, C)
        for e in range(N):
            gone[r + e] = (hg[e] * slope[r + e + D1]).astype(BF16)

    kernel_gradient(gone, D1, D1, xm, VH, HH, D1)
    red1.load(acc, bias)
    red1.start()
    red2.back_y()

    @pl.loop(0, ROWS // 16)
    def _(q):
        r = q * 16
        for e, back in rows_of(pair(gone, r + D1, N, D1, SIDE, D1, w1t), D1):
            live = mask(r + e + VH, HH, SIDE)
            o = gm[r + e + VH, HH : HH + SIDE, :].astype(F32)
            fg_ref[r + e] = (o + jnp.where(live, back, 0.0)).astype(BF16)

    red1.over_y()
    red2.back_xc()
    red1.over_z()
    red2.finish(kg2_ref, bg2_ref)
    red1.back_y()
    red1.back_xc()
    red1.finish(kg1_ref, bg1_ref)

    for a in range(2):
        for name in names:
            sent(a, name)


def on_device(x, gr, bin_valid, k1, b1, k2, b2):
    vmem = pl.BlockSpec(memory_space=pltpu.VMEM)
    smem = pl.BlockSpec(memory_space=pltpu.SMEM)
    hbm = pl.BlockSpec(memory_space=pl.ANY)
    block_out, feature_grad, kg1, bg1, kg2, bg2 = pl.pallas_call(
        main_kernel,
        out_shape=(
            jax.ShapeDtypeStruct((ROWS, SIDE, C), BF16),
            jax.ShapeDtypeStruct((ROWS, SIDE, C), BF16),
            jax.ShapeDtypeStruct((KR, C), F32),
            jax.ShapeDtypeStruct((1, C), F32),
            jax.ShapeDtypeStruct((KR, C), F32),
            jax.ShapeDtypeStruct((1, C), F32),
        ),
        in_specs=[hbm, hbm, smem, vmem, vmem, vmem, vmem],
        out_specs=(vmem,) * 6,
        scratch_shapes=[
            pltpu.VMEM((PR, PC, C), BF16),
            pltpu.VMEM((PR, PC, C), BF16),
            pltpu.VMEM((PR, PC, C), BF16),
            pltpu.VMEM((PR, PC, C), BF16),
            pltpu.VMEM((HR, HC, C), BF16),
            pltpu.VMEM((HR, GC, C), F32),
            pltpu.VMEM((GR, GC, C), BF16),
            pltpu.VMEM((9 * C, C), BF16),
            pltpu.VMEM((9 * C, C), BF16),
            pltpu.VMEM((12 * C, 2 * C), BF16),
            pltpu.VMEM((12 * C, 2 * C), BF16),
            pltpu.VMEM((12 * C, 2 * C), BF16),
            pltpu.VMEM((12 * C, 2 * C), BF16),
            pltpu.VMEM((PC, C), jnp.int32),
            pltpu.VMEM((C, KR), F32),
            pltpu.VMEM((8, C), F32),
            pltpu.VMEM((2, 8, 4, PIECE, C), BF16),
            pltpu.VMEM((2, 7, 4, PIECE, C), BF16),
            pltpu.VMEM((2, 4, PIECE, C), F32),
            pltpu.VMEM((2, 4, PIECE, C), BF16),
            pltpu.VMEM((2, 3, PIECE, C), BF16),
            pltpu.VMEM((2, PIECE, C), BF16),
            pltpu.VMEM((2, 8, PIECE, C), BF16),
            pltpu.VMEM((2, 8, 4, PIECE, C), BF16),
            pltpu.SemaphoreType.DMA((2 * HALO,)),
            pltpu.SemaphoreType.DMA((2 * HALO,)),
            pltpu.SemaphoreType.DMA((2,)),
            pltpu.SemaphoreType.DMA((2 * COPIES,)),
            pltpu.SemaphoreType.DMA((2 * COPIES,)),
        ],
        compiler_params=pltpu.CompilerParams(
            collective_id=0, has_side_effects=True, vmem_limit_bytes=60 * 1024 * 1024
        ),
        name="resblock",
    )(x[0], gr[0], bin_valid, k1.reshape(9, C, C), b1[None], k2.reshape(9, C, C), b2[None])
    return (
        block_out[None],
        feature_grad[None],
        kg1.reshape(3, 3, C, C),
        bg1[0],
        kg2.reshape(3, 3, C, C),
        bg2[0],
    )


def solution(mesh):
    strip = P("tile", "sub", None, None)
    return jax.shard_map(
        on_device,
        mesh=mesh,
        in_specs=(strip, strip, P(), P(), P(), P(), P()),
        out_specs=(strip, strip, P(), P(), P(), P()),
        check_vma=False,
    )
```

```python
import math

import jax
import jax.numpy as jnp
from jax import lax
from jax.experimental import pallas as pl
from jax.experimental.pallas import tpu as pltpu
from jax.sharding import PartitionSpec as P

C = 128
D1 = 8
D2 = 16
DIAGS = 4
TILE_ROWS = 16
TILES = 64
ROWS = 32
SIDE = 128
VH = 24
HH = 32
PR = ROWS + 2 * VH
PC = SIDE + 2 * HH
HR, HC = ROWS + 2 * D2, SIDE + 2 * D2
GR, GC = ROWS + 2 * D1, SIDE + 2 * D1
LOW = D1 + D2
HIGH = (DIAGS - 1) * SIDE - D1 - D2
MESH = pl.DeviceIdType.MESH
F32 = jnp.float32
BF16 = jnp.bfloat16
PIECE = 40
KR = 9 * C
SCALE = 1.0 / math.sqrt(TILES * SIDE * SIDE)
HALO = 26
COPIES = 27


def where_am_i():
    g = lax.axis_index("tile")
    s = lax.axis_index("sub")
    i = lax.rem(g + DIAGS, TILES) // DIAGS
    d = lax.rem(g, DIAGS)
    return g, s, i, d


class Reduction:
    def __init__(self, g, s, bufs, send_sem, recv_sem, first):
        self.s1, self.r1, self.t1, self.s2, self.r2, self.s3, self.r3, self.all = bufs
        self.xc = lax.rem(g, 8)
        self.y = lax.rem(g // 8, 4)
        self.z = (g // 32) * 4 + s
        self.g, self.s = g, s
        self.sems = (send_sem, recv_sem)
        self.first = first
        self.copies = []

    def xc_peer(self, j):
        return {"tile": self.g - self.xc + lax.rem(self.xc + j, 8), "sub": self.s}

    def y_peer(self, j):
        return {"tile": self.g - 8 * self.y + 8 * lax.rem(self.y + j, 4), "sub": self.s}

    def z_peer(self, j):
        other = lax.rem(self.z + j, 8)
        return {"tile": lax.rem(self.g, 32) + 32 * (other // 4), "sub": lax.rem(other, 4)}

    def peers(self):
        return (
            [self.xc_peer(j) for j in range(1, 8)]
            + [self.y_peer(j) for j in range(1, 4)]
            + [self.z_peer(j) for j in range(1, 8)]
        )

    def send(self, src, dst, dev):
        n = self.first + len(self.copies)
        cp = pltpu.make_async_remote_copy(
            src_ref=src,
            dst_ref=dst,
            send_sem=self.sems[0].at[n],
            recv_sem=self.sems[1].at[n],
            device_id=dev,
            device_id_type=MESH,
        )
        cp.start()
        self.copies.append(cp)

    def put(self, row, v):
        v = v.astype(BF16)
        for q in range(0, v.shape[0], 8):
            p, r = divmod(row + q, PIECE)
            self.s1[p // 4, p % 4, r : r + 8, :] = v[q : q + 8]

    def load(self, acc, bias):
        for t in range(9):
            self.put(t * C, acc[:, t * C : (t + 1) * C].T)
        self.put(KR, bias[...])
        self.put(KR + 8, jnp.zeros((32 * PIECE - KR - 8, C), F32))

    def start(self):
        for j in range(1, 8):
            self.send(self.s1.at[lax.rem(self.xc + j, 8)], self.r1.at[j - 1], self.xc_peer(j))

    def over_y(self):
        for j in range(7):
            self.copies[j].wait_recv()
        total = self.s1[self.xc].astype(F32)
        for j in range(7):
            total = total + self.r1[j].astype(F32)
        self.t1[...] = total
        self.s2[...] = total.astype(BF16)
        for j in range(1, 4):
            self.send(self.s2.at[lax.rem(self.y + j, 4)], self.r2.at[j - 1], self.y_peer(j))

    def over_z(self):
        for j in range(3):
            self.copies[7 + j].wait_recv()
        total = self.t1[self.y]
        for j in range(3):
            total = total + self.r2[j].astype(F32)
        self.s3[...] = total.astype(BF16)
        for j in range(1, 8):
            self.send(self.s3, self.r3.at[self.z], self.z_peer(j))
        self.r3[self.z] = self.s3[...]

    def back_y(self):
        for j in range(7):
            self.copies[10 + j].wait_recv()
        total = self.r3[0].astype(F32)
        for j in range(1, 8):
            total = total + self.r3[j].astype(F32)
        self.all[self.xc, self.y] = total.astype(BF16)
        own = self.all.at[self.xc, self.y]
        for j in range(1, 4):
            self.send(own, own, self.y_peer(j))

    def back_xc(self):
        for j in range(3):
            self.copies[17 + j].wait_recv()
        own = self.all.at[self.xc]
        for j in range(1, 8):
            self.send(own, own, self.xc_peer(j))

    def finish(self, kernel_ref, bias_ref):
        for j in range(7):
            self.copies[20 + j].wait_recv()
        for p in range(KR // PIECE + 1):
            n = min(PIECE, KR - p * PIECE)
            kernel_ref[p * PIECE : p * PIECE + n, :] = (
                self.all[p // 4, p % 4, 0:n, :].astype(F32) * SCALE
            )
        p, r = divmod(KR, PIECE)
        tail = self.all[p // 4, p % 4].astype(F32)[r : r + 8]
        bias_ref[...] = jnp.sum(tail, axis=0, keepdims=True) * SCALE
        for cp in self.copies:
            cp.wait_send()


def main_kernel(
    x_ref,
    g_ref,
    valid_ref,
    k1_ref,
    b1_ref,
    k2_ref,
    b2_ref,
    out_ref,
    fg_ref,
    kg_ref,
    xp,
    gp,
    xm,
    gm,
    hid,
    slope,
    gone,
    k1t,
    k2t,
    w1,
    w1t,
    w2,
    w2t,
    dist,
    acc,
    bias,
    s1,
    r1,
    t1,
    s2,
    r2,
    s3,
    r3,
    everything,
    send_sem,
    recv_sem,
    own_sem,
    red_send,
    red_recv,
):
    g, s, i, d = where_am_i()
    bufs = (s1, r1, t1, s2, r2, s3, r3, everything)
    red1, red2 = (
        Reduction(g, s, [b.at[n] for b in bufs], red_send, red_recv, n * COPIES) for n in range(2)
    )
    up_g = jnp.where(s > 0, g, lax.rem(g + TILES - 3, TILES))
    up_s = jnp.where(s > 0, s - 1, 3)
    down_g = jnp.where(s < 3, g, lax.rem(g + 3, TILES))
    down_s = jnp.where(s < 3, s + 1, 0)
    left_g = lax.rem(g + TILES - 1, TILES)
    right_g = lax.rem(g + 1, TILES)
    has_up = (s > 0) | ((d <= 2) & (i > 0))
    has_down = (s < 3) | ((d >= 1) & (i < TILE_ROWS - 1))
    has_left = d > 0
    has_right = d < DIAGS - 1
    sides = {
        "up": (has_up, {"tile": up_g, "sub": up_s}),
        "down": (has_down, {"tile": down_g, "sub": down_s}),
        "left": (has_left, {"tile": left_g, "sub": s}),
        "right": (has_right, {"tile": right_g, "sub": s}),
    }

    own = []
    for n, (src, dst) in enumerate(((x_ref, xp), (g_ref, gp))):
        cp = pltpu.make_async_copy(
            src, dst.at[pl.ds(VH, ROWS), pl.ds(HH, SIDE)], own_sem.at[n]
        )
        cp.start()
        own.append(cp)

    barrier = pltpu.get_barrier_semaphore()
    for has, dev in sides.values():

        @pl.when(has)
        def _():
            pl.semaphore_signal(barrier, inc=1, device_id=dev, device_id_type=MESH)

    for dev in red1.peers():
        pl.semaphore_signal(barrier, inc=1, device_id=dev, device_id_type=MESH)
    count = sum(has.astype(jnp.int32) for has, _ in sides.values())
    pl.semaphore_wait(barrier, count + 17)

    def live_piece(way, p, diag, sub):
        if way == "up":
            return ((diag != 0) | (p >= sub)) & ((diag != DIAGS - 1) | (p < sub))
        return ((diag != 0) | (p > sub)) & ((diag != DIAGS - 1) | (p <= sub))

    above_d, above_s = jnp.where(s > 0, d, d + 1), jnp.where(s > 0, s - 1, 3)
    below_d, below_s = jnp.where(s < 3, d, d - 1), jnp.where(s < 3, s + 1, 0)

    def plan(src, win, parts):
        moves = {}
        for part, first, n in parts:
            top, bottom = VH - first - n, VH + ROWS + first
            for p in range(4):
                c = p * HH
                moves[f"down_{p}{part}"] = (
                    has_down & live_piece("down", p, d, s),
                    has_up & live_piece("down", p, above_d, above_s),
                    sides["down"][1],
                    src.at[pl.ds(ROWS - first - n, n), pl.ds(c, HH)],
                    win.at[pl.ds(top, n), pl.ds(HH + c, HH)],
                )
                moves[f"up_{p}{part}"] = (
                    has_up & live_piece("up", p, d, s),
                    has_down & live_piece("up", p, below_d, below_s),
                    sides["up"][1],
                    src.at[pl.ds(first, n), pl.ds(c, HH)],
                    win.at[pl.ds(bottom, n), pl.ds(HH + c, HH)],
                )
            for name, r in (("top", top), ("bottom", bottom)):
                moves[f"left_{name}{part}"] = (
                    has_left,
                    has_right,
                    sides["left"][1],
                    win.at[pl.ds(r, n), pl.ds(HH, HH)],
                    win.at[pl.ds(r, n), pl.ds(HH + SIDE, HH)],
                )
                moves[f"right_{name}{part}"] = (
                    has_right,
                    has_left,
                    sides["right"][1],
                    win.at[pl.ds(r, n), pl.ds(SIDE, HH)],
                    win.at[pl.ds(r, n), pl.ds(0, HH)],
                )
        moves["left"] = (
            has_left,
            has_right,
            sides["left"][1],
            src.at[pl.ds(0, ROWS), pl.ds(0, HH)],
            win.at[pl.ds(VH, ROWS), pl.ds(HH + SIDE, HH)],
        )
        moves["right"] = (
            has_right,
            has_left,
            sides["right"][1],
            src.at[pl.ds(0, ROWS), pl.ds(SIDE - HH, HH)],
            win.at[pl.ds(VH, ROWS), pl.ds(0, HH)],
        )
        return moves

    plans = (
        plan(x_ref, xp, (("", 0, VH),)),
        plan(g_ref, gp, (("", 0, D2), ("_outer", D2, VH - D2))),
    )

    def copy_of(a, name):
        _, _, dev, src, dst = plans[a][name]
        n = a * HALO + list(plans[a]).index(name)
        return pltpu.make_async_remote_copy(
            src_ref=src,
            dst_ref=dst,
            send_sem=send_sem.at[n],
            recv_sem=recv_sem.at[n],
            device_id=dev,
            device_id_type=MESH,
        )

    def start(a, name):
        @pl.when(plans[a][name][0])
        def _():
            copy_of(a, name).start()

    def sent(a, name):
        @pl.when(plans[a][name][0])
        def _():
            copy_of(a, name).wait_send()

    def arrived(a, name):
        @pl.when(plans[a][name][1])
        def _():
            copy_of(a, name).wait_recv()

    edges = ("down_0", "up_0", "down_3", "up_3")
    middles = ("down_1", "up_1", "down_2", "up_2")
    relays = ("left_top", "right_top", "left_bottom", "right_bottom")
    for a in range(2):
        for name in edges + ("left", "right") + middles:
            start(a, name)
    for name in edges + middles:
        start(1, name + "_outer")

    def relay(a, part=""):
        for name in edges:
            arrived(a, name + part)
        for name in relays:
            start(a, name + part)

    for t in range(9):
        k1t[pl.ds((8 - t) * C, C), :] = k1_ref[t].T
        k2t[pl.ds((8 - t) * C, C), :] = k2_ref[t].T
    zero = jnp.zeros((3 * C, C), BF16)
    k1, k2 = k1_ref[...].reshape(9 * C, C), k2_ref[...].reshape(9 * C, C)
    for dst, src in ((w1, k1), (w2, k2), (w1t, k1t[...]), (w2t, k2t[...])):
        dst[0 : 9 * C, 0:C] = src
        dst[9 * C : 12 * C, 0:C] = zero
        dst[0 : 3 * C, C : 2 * C] = zero
        dst[3 * C : 12 * C, C : 2 * C] = src
    a0 = i * SIDE + s * ROWS - VH
    b0 = (i + d) * SIDE - HH
    n_bins = valid_ref.shape[0]

    @pl.loop(0, PC)
    def _(c):
        b = b0 + c
        ok = (b >= 0) & (b < n_bins) & (valid_ref[jnp.clip(b, 0, n_bins - 1)] > 0)
        dist[pl.ds(c, 1), :] = jnp.full((1, C), jnp.where(ok, b - a0, -100000), jnp.int32)

    def mask(r, c, n):
        a = a0 + r
        last = TILE_ROWS * SIDE - 1
        ok = (a >= 0) & (a <= last) & (valid_ref[jnp.clip(a, 0, last)] > 0)
        far = jnp.where(ok, 0, 1000000)
        here = dist[c : c + n, :]
        return (here >= LOW + r + far) & (here <= HIGH + r)

    def masked(src, r, c, n):
        return jnp.where(mask(r, c, n), src[r, c : c + n, :].astype(F32), 0.0).astype(BF16)

    def gather(ref, r, n, c, m, dil, us):
        parts = []
        for u in us:
            for w in (-1, 0, 1):
                v = ref[pl.ds(r + u * dil, n), c + w * dil : c + w * dil + m, :]
                parts.append(v.reshape(n * m, C))
        return jnp.concatenate(parts, axis=1)

    def taps(ref, r, n, c, m, dil):
        return gather(ref, r, n, c, m, dil, (-1, 0, 1))

    def pair(ref, r, n, c, m, dil, kernel):
        v = gather(ref, r, n, c, m, dil, (-1, 0, 1, 2))
        both = jnp.dot(v, kernel[...], preferred_element_type=F32)
        return both[:, :C].reshape(n, m, C), both[:, C:].reshape(n, m, C)

    def rows_of(both, dil):
        return [(h * dil + k, both[h][k]) for h in range(2) for k in range(both[h].shape[0])]

    N = 8

    relay(0)
    own[0].wait()
    for name in ("left", "right") + middles + relays:
        arrived(0, name)

    @pl.loop(0, PR)
    def _(r):
        xm[r] = masked(xp, r, 0, PC)

    bias1 = jnp.broadcast_to(b1_ref[...], (HC, C))

    @pl.loop(0, HR // 16)
    def _(q):
        r = q * 16
        for e, pre in rows_of(pair(xm, r + D1, N, HH - D2, HC, D1, w1), D1):
            v = pre + bias1
            sig = 1.0 / (1.0 + jnp.exp(-v))
            live = mask(r + e + D1, HH - D2, HC)
            hid[r + e] = jnp.where(live, v * sig, 0.0).astype(BF16)
            sl = jnp.where(live, sig * (1.0 + v * (1.0 - sig)), 0.0)
            slope[r + e] = sl[D1 : D1 + GC]

    own[1].wait()

    @pl.loop(0, ROWS)
    def _(r):
        gm[r + VH, HH : HH + SIDE, :] = masked(gp, r + VH, HH, SIDE)

    step = 8

    def kernel_gradient(cots, row, col, values, vrow, vcol, dil):
        acc[...] = jnp.zeros_like(acc)
        bias[...] = jnp.zeros_like(bias)

        @pl.loop(0, ROWS // step)
        def _(q):
            r = q * step
            cv = cots[pl.ds(r + row, step), col : col + SIDE, :].reshape(step * SIDE, C)
            vv = taps(values, r + vrow, step, vcol, SIDE, dil)
            acc[...] += lax.dot_general(
                cv, vv, (((0,), (0,)), ((), ())), preferred_element_type=F32
            )
            folded = cv.astype(F32).reshape(step * SIDE // 8, 8, C)
            bias[...] += jnp.sum(folded, axis=0)

    kernel_gradient(gm, VH, HH, hid, D2, D2, D2)
    red2.load(acc, bias)
    red2.start()

    bias2 = jnp.broadcast_to(b2_ref[...], (SIDE, C))

    @pl.loop(0, D2 // N)
    def _(q):
        r = q * N
        for e, pre in rows_of(pair(hid, r + D2, N, D2, SIDE, D2, w2), D2):
            live = mask(r + e + VH, HH, SIDE)
            x = xm[r + e + VH, HH : HH + SIDE, :].astype(F32)
            out_ref[r + e] = (x + jnp.where(live, pre + bias2, 0.0)).astype(BF16)

    relay(1)
    for name in ("left", "right") + middles + relays:
        arrived(1, name)

    @pl.loop(VH - D2, VH + ROWS + D2)
    def _(r):
        gm[r] = masked(gp, r, 0, PC)

    @pl.loop(0, D2 // N)
    def _(q):
        r = q * N + D1
        for e, hg in rows_of(pair(gm, r + VH - D1, N, HH - D1, GC, D2, w2t), D2):
            gone[r + e] = (hg * slope[r + e + D1]).astype(BF16)

    kernel_gradient(gone, D1, D1, xm, VH, HH, D1)
    red1.load(acc, bias)
    red1.start()
    relay(1, "_outer")
    red2.over_y()
    for name in middles + relays:
        arrived(1, name + "_outer")

    @pl.loop(0, VH - D2)
    def _(r):
        gm[r] = masked(gp, r, 0, PC)
        gm[r + VH + ROWS + D2] = masked(gp, r + VH + ROWS + D2, 0, PC)

    red2.over_z()

    @pl.loop(0, 2)
    def _(q):
        r = q * (GR - D1)
        v = taps(gm, r + VH - D1, D1, HH - D1, GC, D2)
        hg = jnp.dot(v, k2t[...], preferred_element_type=F32).reshape(D1, GC, C)
        for e in range(D1):
            gone[r + e] = (hg[e] * slope[r + e + D1]).astype(BF16)

    red1.over_y()

    @pl.loop(0, ROWS // 16)
    def _(q):
        r = q * 16
        for e, back in rows_of(pair(gone, r + D1, N, D1, SIDE, D1, w1t), D1):
            live = mask(r + e + VH, HH, SIDE)
            o = gm[r + e + VH, HH : HH + SIDE, :].astype(F32)
            fg_ref[r + e] = (o + jnp.where(live, back, 0.0)).astype(BF16)

    red1.over_z()
    red2.back_y()
    red2.back_xc()
    red1.back_y()
    red1.back_xc()
    red2.finish(kg_ref.at[pl.ds(KR, KR)], kg_ref.at[pl.ds(2 * KR + 8, 1)])
    red1.finish(kg_ref.at[pl.ds(0, KR)], kg_ref.at[pl.ds(2 * KR, 1)])

    for a in range(2):
        for name in plans[a]:
            sent(a, name)


def on_device(x, gr, bin_valid, k1, b1, k2, b2):
    vmem = pl.BlockSpec(memory_space=pltpu.VMEM)
    smem = pl.BlockSpec(memory_space=pltpu.SMEM)
    hbm = pl.BlockSpec(memory_space=pl.ANY)
    block_out, feature_grad, kg = pl.pallas_call(
        main_kernel,
        out_shape=(
            jax.ShapeDtypeStruct((ROWS, SIDE, C), BF16),
            jax.ShapeDtypeStruct((ROWS, SIDE, C), BF16),
            jax.ShapeDtypeStruct((2 * KR + 16, C), F32),
        ),
        in_specs=[hbm, hbm, smem, vmem, vmem, vmem, vmem],
        out_specs=(vmem,) * 3,
        scratch_shapes=[
            pltpu.VMEM((PR, PC, C), BF16),
            pltpu.VMEM((PR, PC, C), BF16),
            pltpu.VMEM((PR, PC, C), BF16),
            pltpu.VMEM((PR, PC, C), BF16),
            pltpu.VMEM((HR, HC, C), BF16),
            pltpu.VMEM((HR, GC, C), F32),
            pltpu.VMEM((GR, GC, C), BF16),
            pltpu.VMEM((9 * C, C), BF16),
            pltpu.VMEM((9 * C, C), BF16),
            pltpu.VMEM((12 * C, 2 * C), BF16),
            pltpu.VMEM((12 * C, 2 * C), BF16),
            pltpu.VMEM((12 * C, 2 * C), BF16),
            pltpu.VMEM((12 * C, 2 * C), BF16),
            pltpu.VMEM((PC, C), jnp.int32),
            pltpu.VMEM((C, KR), F32),
            pltpu.VMEM((8, C), F32),
            pltpu.VMEM((2, 8, 4, PIECE, C), BF16),
            pltpu.VMEM((2, 7, 4, PIECE, C), BF16),
            pltpu.VMEM((2, 4, PIECE, C), F32),
            pltpu.VMEM((2, 4, PIECE, C), BF16),
            pltpu.VMEM((2, 3, PIECE, C), BF16),
            pltpu.VMEM((2, PIECE, C), BF16),
            pltpu.VMEM((2, 8, PIECE, C), BF16),
            pltpu.VMEM((2, 8, 4, PIECE, C), BF16),
            pltpu.SemaphoreType.DMA((2 * HALO,)),
            pltpu.SemaphoreType.DMA((2 * HALO,)),
            pltpu.SemaphoreType.DMA((2,)),
            pltpu.SemaphoreType.DMA((2 * COPIES,)),
            pltpu.SemaphoreType.DMA((2 * COPIES,)),
        ],
        compiler_params=pltpu.CompilerParams(
            collective_id=0, has_side_effects=True, vmem_limit_bytes=60 * 1024 * 1024
        ),
        name="resblock",
    )(x[0], gr[0], bin_valid, k1.reshape(9, C, C), b1[None], k2.reshape(9, C, C), b2[None])
    return (
        block_out[None],
        feature_grad[None],
        kg[:KR].reshape(3, 3, C, C),
        kg[2 * KR],
        kg[KR : 2 * KR].reshape(3, 3, C, C),
        kg[2 * KR + 8],
    )


def solution(mesh):
    strip = P("tile", "sub", None, None)
    return jax.shard_map(
        on_device,
        mesh=mesh,
        in_specs=(strip, strip, P(), P(), P(), P(), P()),
        out_specs=(strip, strip, P(), P(), P(), P()),
        check_vma=False,
    )
```

```python
import math

import jax
import jax.numpy as jnp
from jax import lax
from jax.experimental import pallas as pl
from jax.experimental.pallas import tpu as pltpu
from jax.sharding import PartitionSpec as P

C = 128
D1 = 8
D2 = 16
DIAGS = 4
TILE_ROWS = 16
TILES = 64
ROWS = 32
SIDE = 128
VH = 24
HH = 32
PR = ROWS + 2 * VH
PC = SIDE + 2 * HH
HR, HC = ROWS + 2 * D2, SIDE + 2 * D2
GR, GC = ROWS + 2 * D1, SIDE + 2 * D1
LOW = D1 + D2
HIGH = (DIAGS - 1) * SIDE - D1 - D2
MESH = pl.DeviceIdType.MESH
F32 = jnp.float32
BF16 = jnp.bfloat16
PIECE = 40
KR = 9 * C
SCALE = 1.0 / math.sqrt(TILES * SIDE * SIDE)
HALO = 26
COPIES = 27


def where_am_i():
    g = lax.axis_index("tile")
    s = lax.axis_index("sub")
    i = lax.rem(g + DIAGS, TILES) // DIAGS
    d = lax.rem(g, DIAGS)
    return g, s, i, d


class Reduction:
    def __init__(self, g, s, bufs, send_sem, recv_sem, first):
        self.s1, self.r1, self.t1, self.s2, self.r2, self.s3, self.r3, self.all = bufs
        self.xc = lax.rem(g, 8)
        self.y = lax.rem(g // 8, 4)
        self.z = (g // 32) * 4 + s
        self.g, self.s = g, s
        self.sems = (send_sem, recv_sem)
        self.first = first
        self.copies = []

    def xc_peer(self, j):
        return {"tile": self.g - self.xc + lax.rem(self.xc + j, 8), "sub": self.s}

    def y_peer(self, j):
        return {"tile": self.g - 8 * self.y + 8 * lax.rem(self.y + j, 4), "sub": self.s}

    def z_peer(self, j):
        other = lax.rem(self.z + j, 8)
        return {"tile": lax.rem(self.g, 32) + 32 * (other // 4), "sub": lax.rem(other, 4)}

    def peers(self):
        return (
            [self.xc_peer(j) for j in range(1, 8)]
            + [self.y_peer(j) for j in range(1, 4)]
            + [self.z_peer(j) for j in range(1, 8)]
        )

    def send(self, src, dst, dev):
        n = self.first + len(self.copies)
        cp = pltpu.make_async_remote_copy(
            src_ref=src,
            dst_ref=dst,
            send_sem=self.sems[0].at[n],
            recv_sem=self.sems[1].at[n],
            device_id=dev,
            device_id_type=MESH,
        )
        cp.start()
        self.copies.append(cp)

    def put(self, row, v):
        v = v.astype(BF16)
        for q in range(0, v.shape[0], 8):
            p, r = divmod(row + q, PIECE)
            self.s1[p // 4, p % 4, r : r + 8, :] = v[q : q + 8]

    def load(self, taps, bias):
        for t in range(9):
            self.put(t * C, taps(t))
        self.put(KR, bias[...])
        self.put(KR + 8, jnp.zeros((32 * PIECE - KR - 8, C), F32))

    def start(self):
        for j in range(1, 8):
            self.send(self.s1.at[lax.rem(self.xc + j, 8)], self.r1.at[j - 1], self.xc_peer(j))

    def over_y(self):
        for j in range(7):
            self.copies[j].wait_recv()
        total = self.s1[self.xc].astype(F32)
        for j in range(7):
            total = total + self.r1[j].astype(F32)
        self.t1[...] = total
        self.s2[...] = total.astype(BF16)
        for j in range(1, 4):
            self.send(self.s2.at[lax.rem(self.y + j, 4)], self.r2.at[j - 1], self.y_peer(j))

    def over_z(self):
        for j in range(3):
            self.copies[7 + j].wait_recv()
        total = self.t1[self.y]
        for j in range(3):
            total = total + self.r2[j].astype(F32)
        self.s3[...] = total.astype(BF16)
        for j in range(1, 8):
            self.send(self.s3, self.r3.at[self.z], self.z_peer(j))
        self.r3[self.z] = self.s3[...]

    def back_y(self):
        for j in range(7):
            self.copies[10 + j].wait_recv()
        total = self.r3[0].astype(F32)
        for j in range(1, 8):
            total = total + self.r3[j].astype(F32)
        self.all[self.xc, self.y] = total.astype(BF16)
        own = self.all.at[self.xc, self.y]
        for j in range(1, 4):
            self.send(own, own, self.y_peer(j))

    def back_xc(self):
        for j in range(3):
            self.copies[17 + j].wait_recv()
        own = self.all.at[self.xc]
        for j in range(1, 8):
            self.send(own, own, self.xc_peer(j))

    def finish(self, kernel_ref, bias_ref):
        for j in range(7):
            self.copies[20 + j].wait_recv()
        for p in range(KR // PIECE + 1):
            n = min(PIECE, KR - p * PIECE)
            kernel_ref[p * PIECE : p * PIECE + n, :] = (
                self.all[p // 4, p % 4, 0:n, :].astype(F32) * SCALE
            )
        p, r = divmod(KR, PIECE)
        tail = self.all[p // 4, p % 4].astype(F32)[r : r + 8]
        bias_ref[...] = jnp.sum(tail, axis=0, keepdims=True) * SCALE
        for cp in self.copies:
            cp.wait_send()


def main_kernel(
    x_ref,
    g_ref,
    valid_ref,
    k1_ref,
    b1_ref,
    k2_ref,
    b2_ref,
    out_ref,
    fg_ref,
    kg_ref,
    xp,
    gp,
    xm,
    gm,
    hid,
    slope,
    gone,
    k1t,
    k2t,
    w1,
    w1t,
    w2,
    w2t,
    dist,
    acc,
    bias,
    s1,
    r1,
    t1,
    s2,
    r2,
    s3,
    r3,
    everything,
    send_sem,
    recv_sem,
    own_sem,
    red_send,
    red_recv,
):
    g, s, i, d = where_am_i()
    bufs = (s1, r1, t1, s2, r2, s3, r3, everything)
    red1, red2 = (
        Reduction(g, s, [b.at[n] for b in bufs], red_send, red_recv, n * COPIES) for n in range(2)
    )
    up_g = jnp.where(s > 0, g, lax.rem(g + TILES - 3, TILES))
    up_s = jnp.where(s > 0, s - 1, 3)
    down_g = jnp.where(s < 3, g, lax.rem(g + 3, TILES))
    down_s = jnp.where(s < 3, s + 1, 0)
    left_g = lax.rem(g + TILES - 1, TILES)
    right_g = lax.rem(g + 1, TILES)
    has_up = (s > 0) | ((d <= 2) & (i > 0))
    has_down = (s < 3) | ((d >= 1) & (i < TILE_ROWS - 1))
    has_left = d > 0
    has_right = d < DIAGS - 1
    sides = {
        "up": (has_up, {"tile": up_g, "sub": up_s}),
        "down": (has_down, {"tile": down_g, "sub": down_s}),
        "left": (has_left, {"tile": left_g, "sub": s}),
        "right": (has_right, {"tile": right_g, "sub": s}),
    }

    own = []
    for n, (src, dst) in enumerate(((x_ref, xp), (g_ref, gp))):
        cp = pltpu.make_async_copy(
            src, dst.at[pl.ds(VH, ROWS), pl.ds(HH, SIDE)], own_sem.at[n]
        )
        cp.start()
        own.append(cp)

    barrier = pltpu.get_barrier_semaphore()
    for has, dev in sides.values():

        @pl.when(has)
        def _():
            pl.semaphore_signal(barrier, inc=1, device_id=dev, device_id_type=MESH)

    for dev in red1.peers():
        pl.semaphore_signal(barrier, inc=1, device_id=dev, device_id_type=MESH)
    count = sum(has.astype(jnp.int32) for has, _ in sides.values())
    pl.semaphore_wait(barrier, count + 17)

    def live_piece(way, p, diag, sub):
        if way == "up":
            return ((diag != 0) | (p >= sub)) & ((diag != DIAGS - 1) | (p < sub))
        return ((diag != 0) | (p > sub)) & ((diag != DIAGS - 1) | (p <= sub))

    above_d, above_s = jnp.where(s > 0, d, d + 1), jnp.where(s > 0, s - 1, 3)
    below_d, below_s = jnp.where(s < 3, d, d - 1), jnp.where(s < 3, s + 1, 0)

    def plan(src, win, parts):
        moves = {}
        for part, first, n in parts:
            top, bottom = VH - first - n, VH + ROWS + first
            for p in range(4):
                c = p * HH
                moves[f"down_{p}{part}"] = (
                    has_down & live_piece("down", p, d, s),
                    has_up & live_piece("down", p, above_d, above_s),
                    sides["down"][1],
                    src.at[pl.ds(ROWS - first - n, n), pl.ds(c, HH)],
                    win.at[pl.ds(top, n), pl.ds(HH + c, HH)],
                )
                moves[f"up_{p}{part}"] = (
                    has_up & live_piece("up", p, d, s),
                    has_down & live_piece("up", p, below_d, below_s),
                    sides["up"][1],
                    src.at[pl.ds(first, n), pl.ds(c, HH)],
                    win.at[pl.ds(bottom, n), pl.ds(HH + c, HH)],
                )
            for name, r in (("top", top), ("bottom", bottom)):
                moves[f"left_{name}{part}"] = (
                    has_left,
                    has_right,
                    sides["left"][1],
                    win.at[pl.ds(r, n), pl.ds(HH, HH)],
                    win.at[pl.ds(r, n), pl.ds(HH + SIDE, HH)],
                )
                moves[f"right_{name}{part}"] = (
                    has_right,
                    has_left,
                    sides["right"][1],
                    win.at[pl.ds(r, n), pl.ds(SIDE, HH)],
                    win.at[pl.ds(r, n), pl.ds(0, HH)],
                )
        moves["left"] = (
            has_left,
            has_right,
            sides["left"][1],
            src.at[pl.ds(0, ROWS), pl.ds(0, HH)],
            win.at[pl.ds(VH, ROWS), pl.ds(HH + SIDE, HH)],
        )
        moves["right"] = (
            has_right,
            has_left,
            sides["right"][1],
            src.at[pl.ds(0, ROWS), pl.ds(SIDE - HH, HH)],
            win.at[pl.ds(VH, ROWS), pl.ds(0, HH)],
        )
        return moves

    plans = (
        plan(x_ref, xp, (("", 0, D1), ("_outer", D1, VH - D1))),
        plan(g_ref, gp, (("", 0, D2), ("_outer", D2, VH - D2))),
    )

    def copy_of(a, name):
        _, _, dev, src, dst = plans[a][name]
        n = a * HALO + list(plans[a]).index(name)
        return pltpu.make_async_remote_copy(
            src_ref=src,
            dst_ref=dst,
            send_sem=send_sem.at[n],
            recv_sem=recv_sem.at[n],
            device_id=dev,
            device_id_type=MESH,
        )

    def start(a, name):
        @pl.when(plans[a][name][0])
        def _():
            copy_of(a, name).start()

    def sent(a, name):
        @pl.when(plans[a][name][0])
        def _():
            copy_of(a, name).wait_send()

    def arrived(a, name):
        @pl.when(plans[a][name][1])
        def _():
            copy_of(a, name).wait_recv()

    edges = ("down_0", "up_0", "down_3", "up_3")
    middles = ("down_1", "up_1", "down_2", "up_2")
    relays = ("left_top", "right_top", "left_bottom", "right_bottom")
    for a in range(2):
        for name in edges + ("left", "right") + middles:
            start(a, name)
    for name in edges + middles:
        start(1, name + "_outer")

    def relay(a, part=""):
        for name in edges:
            arrived(a, name + part)
        for name in relays:
            start(a, name + part)

    for t in range(9):
        k1t[pl.ds((8 - t) * C, C), :] = k1_ref[t].T
        k2t[pl.ds((8 - t) * C, C), :] = k2_ref[t].T
    zero = jnp.zeros((3 * C, C), BF16)
    k1, k2 = k1_ref[...].reshape(9 * C, C), k2_ref[...].reshape(9 * C, C)
    for dst, src in ((w1, k1), (w2, k2), (w1t, k1t[...]), (w2t, k2t[...])):
        dst[0 : 9 * C, 0:C] = src
        dst[9 * C : 12 * C, 0:C] = zero
        dst[0 : 3 * C, C : 2 * C] = zero
        dst[3 * C : 12 * C, C : 2 * C] = src
    a0 = i * SIDE + s * ROWS - VH
    b0 = (i + d) * SIDE - HH
    n_bins = valid_ref.shape[0]

    @pl.loop(0, PC)
    def _(c):
        b = b0 + c
        ok = (b >= 0) & (b < n_bins) & (valid_ref[jnp.clip(b, 0, n_bins - 1)] > 0)
        dist[pl.ds(c, 1), :] = jnp.full((1, C), jnp.where(ok, b - a0, -100000), jnp.int32)

    def mask(r, c, n):
        a = a0 + r
        last = TILE_ROWS * SIDE - 1
        ok = (a >= 0) & (a <= last) & (valid_ref[jnp.clip(a, 0, last)] > 0)
        far = jnp.where(ok, 0, 1000000)
        here = dist[c : c + n, :]
        return (here >= LOW + r + far) & (here <= HIGH + r)

    def masked(src, r, c, n):
        return jnp.where(mask(r, c, n), src[r, c : c + n, :].astype(F32), 0.0).astype(BF16)

    def gather(ref, r, n, c, m, dil, us):
        parts = []
        for u in us:
            for w in (-1, 0, 1):
                v = ref[pl.ds(r + u * dil, n), c + w * dil : c + w * dil + m, :]
                parts.append(v.reshape(n * m, C))
        return jnp.concatenate(parts, axis=1)

    def taps(ref, r, n, c, m, dil):
        return gather(ref, r, n, c, m, dil, (-1, 0, 1))

    def pair(ref, r, n, c, m, dil, kernel):
        v = gather(ref, r, n, c, m, dil, (-1, 0, 1, 2))
        both = jnp.dot(v, kernel[...], preferred_element_type=F32)
        return both[:, :C].reshape(n, m, C), both[:, C:].reshape(n, m, C)

    def rows_of(both, dil):
        return [(h * dil + k, both[h][k]) for h in range(2) for k in range(both[h].shape[0])]

    N = 8

    bias1 = jnp.broadcast_to(b1_ref[...], (HC, C))

    def hidden_rows(r):
        for e, pre in rows_of(pair(xm, r + D1, N, HH - D2, HC, D1, w1), D1):
            v = pre + bias1
            sig = 1.0 / (1.0 + jnp.exp(-v))
            live = mask(r + e + D1, HH - D2, HC)
            hid[r + e] = jnp.where(live, v * sig, 0.0).astype(BF16)
            sl = jnp.where(live, sig * (1.0 + v * (1.0 - sig)), 0.0)
            slope[r + e] = sl[D1 : D1 + GC]

    relay(0)
    own[0].wait()
    for name in ("left", "right") + middles + relays:
        arrived(0, name)

    @pl.loop(VH - D1, VH + ROWS + D1)
    def _(r):
        xm[r] = masked(xp, r, 0, PC)

    @pl.loop(0, ROWS // 16)
    def _(q):
        hidden_rows(D2 + q * 16)

    relay(1)
    own[1].wait()
    for name in ("left", "right") + middles + relays:
        arrived(1, name)

    @pl.loop(VH - D2, VH + ROWS + D2)
    def _(r):
        gm[r] = masked(gp, r, 0, PC)

    step = 8

    def kernel_gradient(mine, row, col, shifted, srow, scol, dil, cots, crow, ccol):
        acc[...] = jnp.zeros_like(acc)
        bias[...] = jnp.zeros_like(bias)

        @pl.loop(0, ROWS // step)
        def _(q):
            r = q * step
            mv = mine[pl.ds(r + row, step), col : col + SIDE, :].reshape(step * SIDE, C)
            sv = taps(shifted, r + srow, step, scol, SIDE, dil)
            acc[...] += lax.dot_general(
                mv, sv, (((0,), (0,)), ((), ())), preferred_element_type=F32
            )
            cv = cots[pl.ds(r + crow, step), ccol : ccol + SIDE, :].astype(F32)
            bias[...] += jnp.sum(cv.reshape(step * SIDE // 8, 8, C), axis=0)

    kernel_gradient(hid, D2, D2, gm, VH, HH, D2, gm, VH, HH)
    red2.load(lambda t: acc[:, (8 - t) * C : (9 - t) * C], bias)
    red2.start()

    @pl.loop(0, D2 // N)
    def _(q):
        r = q * N + D1
        for e, hg in rows_of(pair(gm, r + VH - D1, N, HH - D1, GC, D2, w2t), D2):
            gone[r + e] = (hg * slope[r + e + D1]).astype(BF16)

    kernel_gradient(gone, D1, D1, xm, VH, HH, D1, gone, D1, D1)
    red1.load(lambda t: acc[:, t * C : (t + 1) * C].T, bias)
    red1.start()
    for name in edges:
        start(0, name + "_outer")

    relay(1, "_outer")
    red2.over_y()
    red1.over_y()
    red2.over_z()
    red1.over_z()
    for name in middles:
        start(0, name + "_outer")
    for name in middles + relays:
        arrived(1, name + "_outer")

    @pl.loop(0, VH - D2)
    def _(r):
        gm[r] = masked(gp, r, 0, PC)
        gm[r + VH + ROWS + D2] = masked(gp, r + VH + ROWS + D2, 0, PC)

    relay(0, "_outer")
    red2.back_y()
    red1.back_y()
    red2.back_xc()
    red1.back_xc()
    for name in middles + relays:
        arrived(0, name + "_outer")

    @pl.loop(0, VH - D1)
    def _(r):
        xm[r] = masked(xp, r, 0, PC)
        xm[r + VH + ROWS + D1] = masked(xp, r + VH + ROWS + D1, 0, PC)

    @pl.loop(0, 2)
    def _(q):
        hidden_rows(q * (HR - D2))

    bias2 = jnp.broadcast_to(b2_ref[...], (SIDE, C))

    @pl.loop(0, D2 // N)
    def _(q):
        r = q * N
        for e, pre in rows_of(pair(hid, r + D2, N, D2, SIDE, D2, w2), D2):
            live = mask(r + e + VH, HH, SIDE)
            x = xm[r + e + VH, HH : HH + SIDE, :].astype(F32)
            out_ref[r + e] = (x + jnp.where(live, pre + bias2, 0.0)).astype(BF16)

    @pl.loop(0, 2)
    def _(q):
        r = q * (GR - D1)
        v = taps(gm, r + VH - D1, D1, HH - D1, GC, D2)
        hg = jnp.dot(v, k2t[...], preferred_element_type=F32).reshape(D1, GC, C)
        for e in range(D1):
            gone[r + e] = (hg[e] * slope[r + e + D1]).astype(BF16)

    @pl.loop(0, ROWS // 16)
    def _(q):
        r = q * 16
        for e, back in rows_of(pair(gone, r + D1, N, D1, SIDE, D1, w1t), D1):
            live = mask(r + e + VH, HH, SIDE)
            o = gm[r + e + VH, HH : HH + SIDE, :].astype(F32)
            fg_ref[r + e] = (o + jnp.where(live, back, 0.0)).astype(BF16)

    red2.finish(kg_ref.at[pl.ds(KR, KR)], kg_ref.at[pl.ds(2 * KR + 8, 1)])
    red1.finish(kg_ref.at[pl.ds(0, KR)], kg_ref.at[pl.ds(2 * KR, 1)])

    for a in range(2):
        for name in plans[a]:
            sent(a, name)


def on_device(x, gr, bin_valid, k1, b1, k2, b2):
    vmem = pl.BlockSpec(memory_space=pltpu.VMEM)
    smem = pl.BlockSpec(memory_space=pltpu.SMEM)
    hbm = pl.BlockSpec(memory_space=pl.ANY)
    block_out, feature_grad, kg = pl.pallas_call(
        main_kernel,
        out_shape=(
            jax.ShapeDtypeStruct((ROWS, SIDE, C), BF16),
            jax.ShapeDtypeStruct((ROWS, SIDE, C), BF16),
            jax.ShapeDtypeStruct((2 * KR + 16, C), F32),
        ),
        in_specs=[hbm, hbm, smem, vmem, vmem, vmem, vmem],
        out_specs=(vmem,) * 3,
        scratch_shapes=[
            pltpu.VMEM((PR, PC, C), BF16),
            pltpu.VMEM((PR, PC, C), BF16),
            pltpu.VMEM((PR, PC, C), BF16),
            pltpu.VMEM((PR, PC, C), BF16),
            pltpu.VMEM((HR, HC, C), BF16),
            pltpu.VMEM((HR, GC, C), F32),
            pltpu.VMEM((GR, GC, C), BF16),
            pltpu.VMEM((9 * C, C), BF16),
            pltpu.VMEM((9 * C, C), BF16),
            pltpu.VMEM((12 * C, 2 * C), BF16),
            pltpu.VMEM((12 * C, 2 * C), BF16),
            pltpu.VMEM((12 * C, 2 * C), BF16),
            pltpu.VMEM((12 * C, 2 * C), BF16),
            pltpu.VMEM((PC, C), jnp.int32),
            pltpu.VMEM((C, KR), F32),
            pltpu.VMEM((8, C), F32),
            pltpu.VMEM((2, 8, 4, PIECE, C), BF16),
            pltpu.VMEM((2, 7, 4, PIECE, C), BF16),
            pltpu.VMEM((2, 4, PIECE, C), F32),
            pltpu.VMEM((2, 4, PIECE, C), BF16),
            pltpu.VMEM((2, 3, PIECE, C), BF16),
            pltpu.VMEM((2, PIECE, C), BF16),
            pltpu.VMEM((2, 8, PIECE, C), BF16),
            pltpu.VMEM((2, 8, 4, PIECE, C), BF16),
            pltpu.SemaphoreType.DMA((2 * HALO,)),
            pltpu.SemaphoreType.DMA((2 * HALO,)),
            pltpu.SemaphoreType.DMA((2,)),
            pltpu.SemaphoreType.DMA((2 * COPIES,)),
            pltpu.SemaphoreType.DMA((2 * COPIES,)),
        ],
        compiler_params=pltpu.CompilerParams(
            collective_id=0, has_side_effects=True, vmem_limit_bytes=60 * 1024 * 1024
        ),
        name="resblock",
    )(x[0], gr[0], bin_valid, k1.reshape(9, C, C), b1[None], k2.reshape(9, C, C), b2[None])
    return (
        block_out[None],
        feature_grad[None],
        kg[:KR].reshape(3, 3, C, C),
        kg[2 * KR],
        kg[KR : 2 * KR].reshape(3, 3, C, C),
        kg[2 * KR + 8],
    )


def solution(mesh):
    strip = P("tile", "sub", None, None)
    return jax.shard_map(
        on_device,
        mesh=mesh,
        in_specs=(strip, strip, P(), P(), P(), P(), P()),
        out_specs=(strip, strip, P(), P(), P(), P()),
        check_vma=False,
    )
```

```python
import math

import jax
import jax.numpy as jnp
from jax import lax
from jax.experimental import pallas as pl
from jax.experimental.pallas import tpu as pltpu
from jax.sharding import PartitionSpec as P

C = 128
D1 = 8
D2 = 16
DIAGS = 4
TILE_ROWS = 16
TILES = 64
ROWS = 32
SIDE = 128
VH = 24
HH = 32
PR = ROWS + 2 * VH
PC = SIDE + 2 * HH
HR, HC = ROWS + 2 * D2, SIDE + 2 * D2
GR, GC = ROWS + 2 * D1, SIDE + 2 * D1
LOW = D1 + D2
HIGH = (DIAGS - 1) * SIDE - D1 - D2
MESH = pl.DeviceIdType.MESH
F32 = jnp.float32
BF16 = jnp.bfloat16
PIECE = 40
KR = 9 * C
SCALE = 1.0 / math.sqrt(TILES * SIDE * SIDE)
HALO = 38
COPIES = 27


def where_am_i():
    g = lax.axis_index("tile")
    s = lax.axis_index("sub")
    i = lax.rem(g + DIAGS, TILES) // DIAGS
    d = lax.rem(g, DIAGS)
    return g, s, i, d


class Reduction:
    def __init__(self, g, s, bufs, send_sem, recv_sem, first):
        self.s1, self.r1, self.t1, self.s2, self.r2, self.s3, self.r3, self.all = bufs
        self.xc = lax.rem(g, 8)
        self.y = lax.rem(g // 8, 4)
        self.z = (g // 32) * 4 + s
        self.g, self.s = g, s
        self.sems = (send_sem, recv_sem)
        self.first = first
        self.copies = []

    def xc_peer(self, j):
        return {"tile": self.g - self.xc + lax.rem(self.xc + j, 8), "sub": self.s}

    def y_peer(self, j):
        return {"tile": self.g - 8 * self.y + 8 * lax.rem(self.y + j, 4), "sub": self.s}

    def z_peer(self, j):
        other = lax.rem(self.z + j, 8)
        return {"tile": lax.rem(self.g, 32) + 32 * (other // 4), "sub": lax.rem(other, 4)}

    def peers(self):
        return (
            [self.xc_peer(j) for j in range(1, 8)]
            + [self.y_peer(j) for j in range(1, 4)]
            + [self.z_peer(j) for j in range(1, 8)]
        )

    def send(self, src, dst, dev):
        n = self.first + len(self.copies)
        cp = pltpu.make_async_remote_copy(
            src_ref=src,
            dst_ref=dst,
            send_sem=self.sems[0].at[n],
            recv_sem=self.sems[1].at[n],
            device_id=dev,
            device_id_type=MESH,
        )
        cp.start()
        self.copies.append(cp)

    def put(self, row, v):
        v = v.astype(BF16)
        for q in range(0, v.shape[0], 8):
            p, r = divmod(row + q, PIECE)
            self.s1[p // 4, p % 4, r : r + 8, :] = v[q : q + 8]

    def load(self, taps, bias):
        for t in range(9):
            self.put(t * C, taps(t))
        self.put(KR, bias[...])
        self.put(KR + 8, jnp.zeros((32 * PIECE - KR - 8, C), F32))

    def start(self):
        for j in range(1, 8):
            self.send(self.s1.at[lax.rem(self.xc + j, 8)], self.r1.at[j - 1], self.xc_peer(j))

    def over_y(self):
        for j in range(7):
            self.copies[j].wait_recv()
        total = self.s1[self.xc].astype(F32)
        for j in range(7):
            total = total + self.r1[j].astype(F32)
        self.t1[...] = total
        self.s2[...] = total.astype(BF16)
        for j in range(1, 4):
            self.send(self.s2.at[lax.rem(self.y + j, 4)], self.r2.at[j - 1], self.y_peer(j))

    def over_z(self):
        for j in range(3):
            self.copies[7 + j].wait_recv()
        total = self.t1[self.y]
        for j in range(3):
            total = total + self.r2[j].astype(F32)
        self.s3[...] = total.astype(BF16)
        for j in range(1, 8):
            self.send(self.s3, self.r3.at[self.z], self.z_peer(j))
        self.r3[self.z] = self.s3[...]

    def back_y(self):
        for j in range(7):
            self.copies[10 + j].wait_recv()
        total = self.r3[0].astype(F32)
        for j in range(1, 8):
            total = total + self.r3[j].astype(F32)
        self.all[self.xc, self.y] = total.astype(BF16)
        own = self.all.at[self.xc, self.y]
        for j in range(1, 4):
            self.send(own, own, self.y_peer(j))

    def back_xc(self):
        for j in range(3):
            self.copies[17 + j].wait_recv()
        own = self.all.at[self.xc]
        for j in range(1, 8):
            self.send(own, own, self.xc_peer(j))

    def finish(self, kernel_ref, bias_ref):
        for j in range(7):
            self.copies[20 + j].wait_recv()
        for p in range(KR // PIECE + 1):
            n = min(PIECE, KR - p * PIECE)
            kernel_ref[p * PIECE : p * PIECE + n, :] = (
                self.all[p // 4, p % 4, 0:n, :].astype(F32) * SCALE
            )
        p, r = divmod(KR, PIECE)
        tail = self.all[p // 4, p % 4].astype(F32)[r : r + 8]
        bias_ref[...] = jnp.sum(tail, axis=0, keepdims=True) * SCALE
        for cp in self.copies:
            cp.wait_send()


def main_kernel(
    x_ref,
    g_ref,
    valid_ref,
    k1_ref,
    b1_ref,
    k2_ref,
    b2_ref,
    out_ref,
    fg_ref,
    kg_ref,
    xp,
    gp,
    xm,
    gm,
    hid,
    slope,
    gone,
    k1t,
    k2t,
    w1,
    w1t,
    w2,
    w2t,
    dist,
    acc,
    bias,
    s1,
    r1,
    t1,
    s2,
    r2,
    s3,
    r3,
    everything,
    send_sem,
    recv_sem,
    own_sem,
    red_send,
    red_recv,
):
    g, s, i, d = where_am_i()
    bufs = (s1, r1, t1, s2, r2, s3, r3, everything)
    red1, red2 = (
        Reduction(g, s, [b.at[n] for b in bufs], red_send, red_recv, n * COPIES) for n in range(2)
    )
    up_g = jnp.where(s > 0, g, lax.rem(g + TILES - 3, TILES))
    up_s = jnp.where(s > 0, s - 1, 3)
    down_g = jnp.where(s < 3, g, lax.rem(g + 3, TILES))
    down_s = jnp.where(s < 3, s + 1, 0)
    left_g = lax.rem(g + TILES - 1, TILES)
    right_g = lax.rem(g + 1, TILES)
    has_up = (s > 0) | ((d <= 2) & (i > 0))
    has_down = (s < 3) | ((d >= 1) & (i < TILE_ROWS - 1))
    has_left = d > 0
    has_right = d < DIAGS - 1
    sides = {
        "up": (has_up, {"tile": up_g, "sub": up_s}),
        "down": (has_down, {"tile": down_g, "sub": down_s}),
        "left": (has_left, {"tile": left_g, "sub": s}),
        "right": (has_right, {"tile": right_g, "sub": s}),
    }

    own = []
    for n, (src, dst) in enumerate(((x_ref, xp), (g_ref, gp))):
        cp = pltpu.make_async_copy(
            src, dst.at[pl.ds(VH, ROWS), pl.ds(HH, SIDE)], own_sem.at[n]
        )
        cp.start()
        own.append(cp)

    barrier = pltpu.get_barrier_semaphore()
    for has, dev in sides.values():

        @pl.when(has)
        def _():
            pl.semaphore_signal(barrier, inc=1, device_id=dev, device_id_type=MESH)

    for dev in red1.peers():
        pl.semaphore_signal(barrier, inc=1, device_id=dev, device_id_type=MESH)
    count = sum(has.astype(jnp.int32) for has, _ in sides.values())
    pl.semaphore_wait(barrier, count + 17)

    def live_piece(way, p, diag, sub):
        if way == "up":
            return ((diag != 0) | (p >= sub)) & ((diag != DIAGS - 1) | (p < sub))
        return ((diag != 0) | (p > sub)) & ((diag != DIAGS - 1) | (p <= sub))

    above_d, above_s = jnp.where(s > 0, d, d + 1), jnp.where(s > 0, s - 1, 3)
    below_d, below_s = jnp.where(s < 3, d, d - 1), jnp.where(s < 3, s + 1, 0)

    def plan(src, win, parts):
        moves = {}
        for part, first, n in parts:
            top, bottom = VH - first - n, VH + ROWS + first
            for p in range(4):
                c = p * HH
                moves[f"down_{p}{part}"] = (
                    has_down & live_piece("down", p, d, s),
                    has_up & live_piece("down", p, above_d, above_s),
                    sides["down"][1],
                    src.at[pl.ds(ROWS - first - n, n), pl.ds(c, HH)],
                    win.at[pl.ds(top, n), pl.ds(HH + c, HH)],
                )
                moves[f"up_{p}{part}"] = (
                    has_up & live_piece("up", p, d, s),
                    has_down & live_piece("up", p, below_d, below_s),
                    sides["up"][1],
                    src.at[pl.ds(first, n), pl.ds(c, HH)],
                    win.at[pl.ds(bottom, n), pl.ds(HH + c, HH)],
                )
            for name, r in (("top", top), ("bottom", bottom)):
                moves[f"left_{name}{part}"] = (
                    has_left,
                    has_right,
                    sides["left"][1],
                    win.at[pl.ds(r, n), pl.ds(HH, HH)],
                    win.at[pl.ds(r, n), pl.ds(HH + SIDE, HH)],
                )
                moves[f"right_{name}{part}"] = (
                    has_right,
                    has_left,
                    sides["right"][1],
                    win.at[pl.ds(r, n), pl.ds(SIDE, HH)],
                    win.at[pl.ds(r, n), pl.ds(0, HH)],
                )
        moves["left"] = (
            has_left,
            has_right,
            sides["left"][1],
            src.at[pl.ds(0, ROWS), pl.ds(0, HH)],
            win.at[pl.ds(VH, ROWS), pl.ds(HH + SIDE, HH)],
        )
        moves["right"] = (
            has_right,
            has_left,
            sides["right"][1],
            src.at[pl.ds(0, ROWS), pl.ds(SIDE - HH, HH)],
            win.at[pl.ds(VH, ROWS), pl.ds(0, HH)],
        )
        return moves

    plans = (
        plan(x_ref, xp, (("", 0, D1), ("_mid", D1, D1), ("_outer", 2 * D1, D1))),
        plan(g_ref, gp, (("", 0, D2), ("_outer", D2, VH - D2))),
    )

    def copy_of(a, name):
        _, _, dev, src, dst = plans[a][name]
        n = a * HALO + list(plans[a]).index(name)
        return pltpu.make_async_remote_copy(
            src_ref=src,
            dst_ref=dst,
            send_sem=send_sem.at[n],
            recv_sem=recv_sem.at[n],
            device_id=dev,
            device_id_type=MESH,
        )

    def start(a, name):
        @pl.when(plans[a][name][0])
        def _():
            copy_of(a, name).start()

    def sent(a, name):
        @pl.when(plans[a][name][0])
        def _():
            copy_of(a, name).wait_send()

    def arrived(a, name):
        @pl.when(plans[a][name][1])
        def _():
            copy_of(a, name).wait_recv()

    edges = ("down_0", "up_0", "down_3", "up_3")
    middles = ("down_1", "up_1", "down_2", "up_2")
    relays = ("left_top", "right_top", "left_bottom", "right_bottom")
    for a in range(2):
        for name in edges + ("left", "right") + middles:
            start(a, name)
    for name in edges + middles:
        start(1, name + "_outer")

    def relay(a, part=""):
        for name in edges:
            arrived(a, name + part)
        for name in relays:
            start(a, name + part)

    for t in range(9):
        k1t[pl.ds((8 - t) * C, C), :] = k1_ref[t].T
        k2t[pl.ds((8 - t) * C, C), :] = k2_ref[t].T
    zero = jnp.zeros((3 * C, C), BF16)
    k1, k2 = k1_ref[...].reshape(9 * C, C), k2_ref[...].reshape(9 * C, C)
    for dst, src in ((w1, k1), (w2, k2), (w1t, k1t[...]), (w2t, k2t[...])):
        dst[0 : 9 * C, 0:C] = src
        dst[9 * C : 12 * C, 0:C] = zero
        dst[0 : 3 * C, C : 2 * C] = zero
        dst[3 * C : 12 * C, C : 2 * C] = src
    a0 = i * SIDE + s * ROWS - VH
    b0 = (i + d) * SIDE - HH
    n_bins = valid_ref.shape[0]

    @pl.loop(0, PC)
    def _(c):
        b = b0 + c
        ok = (b >= 0) & (b < n_bins) & (valid_ref[jnp.clip(b, 0, n_bins - 1)] > 0)
        dist[pl.ds(c, 1), :] = jnp.full((1, C), jnp.where(ok, b - a0, -100000), jnp.int32)

    def mask(r, c, n):
        a = a0 + r
        last = TILE_ROWS * SIDE - 1
        ok = (a >= 0) & (a <= last) & (valid_ref[jnp.clip(a, 0, last)] > 0)
        far = jnp.where(ok, 0, 1000000)
        here = dist[c : c + n, :]
        return (here >= LOW + r + far) & (here <= HIGH + r)

    def masked(src, r, c, n):
        return jnp.where(mask(r, c, n), src[r, c : c + n, :].astype(F32), 0.0).astype(BF16)

    def gather(ref, r, n, c, m, dil, us):
        parts = []
        for u in us:
            for w in (-1, 0, 1):
                v = ref[pl.ds(r + u * dil, n), c + w * dil : c + w * dil + m, :]
                parts.append(v.reshape(n * m, C))
        return jnp.concatenate(parts, axis=1)

    def taps(ref, r, n, c, m, dil):
        return gather(ref, r, n, c, m, dil, (-1, 0, 1))

    def pair(ref, r, n, c, m, dil, kernel):
        v = gather(ref, r, n, c, m, dil, (-1, 0, 1, 2))
        both = jnp.dot(v, kernel[...], preferred_element_type=F32)
        return both[:, :C].reshape(n, m, C), both[:, C:].reshape(n, m, C)

    def rows_of(both, dil):
        return [(h * dil + k, both[h][k]) for h in range(2) for k in range(both[h].shape[0])]

    N = 8

    bias1 = jnp.broadcast_to(b1_ref[...], (HC, C))

    def hidden_rows(r):
        keep_hidden(r, rows_of(pair(xm, r + D1, N, HH - D2, HC, D1, w1), D1))

    def hidden_strip(r):
        v = taps(xm, r + D1, N, HH - D2, HC, D1)
        pre = jnp.dot(v, k1_ref[...].reshape(9 * C, C), preferred_element_type=F32)
        keep_hidden(r, list(enumerate(pre.reshape(N, HC, C))))

    def keep_hidden(r, rows):
        for e, pre in rows:
            v = pre + bias1
            sig = 1.0 / (1.0 + jnp.exp(-v))
            live = mask(r + e + D1, HH - D2, HC)
            hid[r + e] = jnp.where(live, v * sig, 0.0).astype(BF16)
            sl = jnp.where(live, sig * (1.0 + v * (1.0 - sig)), 0.0)
            slope[r + e] = sl[D1 : D1 + GC]

    relay(0)
    own[0].wait()
    for name in ("left", "right") + middles + relays:
        arrived(0, name)

    @pl.loop(VH - D1, VH + ROWS + D1)
    def _(r):
        xm[r] = masked(xp, r, 0, PC)

    @pl.loop(0, ROWS // 16)
    def _(q):
        hidden_rows(D2 + q * 16)

    relay(1)
    own[1].wait()
    for name in ("left", "right") + middles + relays:
        arrived(1, name)

    @pl.loop(VH - D2, VH + ROWS + D2)
    def _(r):
        gm[r] = masked(gp, r, 0, PC)

    step = 8

    def kernel_gradient(mine, row, col, shifted, srow, scol, dil, cots, crow, ccol):
        acc[...] = jnp.zeros_like(acc)
        bias[...] = jnp.zeros_like(bias)

        @pl.loop(0, ROWS // step)
        def _(q):
            r = q * step
            mv = mine[pl.ds(r + row, step), col : col + SIDE, :].reshape(step * SIDE, C)
            sv = taps(shifted, r + srow, step, scol, SIDE, dil)
            acc[...] += lax.dot_general(
                mv, sv, (((0,), (0,)), ((), ())), preferred_element_type=F32
            )
            cv = cots[pl.ds(r + crow, step), ccol : ccol + SIDE, :].astype(F32)
            bias[...] += jnp.sum(cv.reshape(step * SIDE // 8, 8, C), axis=0)

    kernel_gradient(hid, D2, D2, gm, VH, HH, D2, gm, VH, HH)
    red2.load(lambda t: acc[:, (8 - t) * C : (9 - t) * C], bias)
    red2.start()

    @pl.loop(0, D2 // N)
    def _(q):
        r = q * N + D1
        for e, hg in rows_of(pair(gm, r + VH - D1, N, HH - D1, GC, D2, w2t), D2):
            gone[r + e] = (hg * slope[r + e + D1]).astype(BF16)

    kernel_gradient(gone, D1, D1, xm, VH, HH, D1, gone, D1, D1)
    red1.load(lambda t: acc[:, t * C : (t + 1) * C].T, bias)
    red1.start()
    for name in edges + middles:
        start(0, name + "_mid")

    relay(1, "_outer")
    red2.over_y()
    red1.over_y()
    red2.over_z()
    red1.over_z()
    for name in edges + middles:
        start(0, name + "_outer")
    for name in middles + relays:
        arrived(1, name + "_outer")

    @pl.loop(0, VH - D2)
    def _(r):
        gm[r] = masked(gp, r, 0, PC)
        gm[r + VH + ROWS + D2] = masked(gp, r + VH + ROWS + D2, 0, PC)

    relay(0, "_mid")
    red2.back_y()
    red1.back_y()
    for name in middles + relays:
        arrived(0, name + "_mid")

    @pl.loop(D1, 2 * D1)
    def _(r):
        xm[r] = masked(xp, r, 0, PC)
        xm[r + ROWS + 3 * D1] = masked(xp, r + ROWS + 3 * D1, 0, PC)

    @pl.loop(0, 2)
    def _(q):
        hidden_strip(D1 + q * (ROWS + D1))

    red2.back_xc()
    red1.back_xc()

    @pl.loop(0, 2)
    def _(q):
        r = q * (GR - D1)
        v = taps(gm, r + VH - D1, D1, HH - D1, GC, D2)
        hg = jnp.dot(v, k2t[...], preferred_element_type=F32).reshape(D1, GC, C)
        for e in range(D1):
            gone[r + e] = (hg[e] * slope[r + e + D1]).astype(BF16)

    relay(0, "_outer")

    @pl.loop(0, ROWS // 16)
    def _(q):
        r = q * 16
        for e, back in rows_of(pair(gone, r + D1, N, D1, SIDE, D1, w1t), D1):
            live = mask(r + e + VH, HH, SIDE)
            o = gm[r + e + VH, HH : HH + SIDE, :].astype(F32)
            fg_ref[r + e] = (o + jnp.where(live, back, 0.0)).astype(BF16)

    for name in middles + relays:
        arrived(0, name + "_outer")

    @pl.loop(0, D1)
    def _(r):
        xm[r] = masked(xp, r, 0, PC)
        xm[r + PR - D1] = masked(xp, r + PR - D1, 0, PC)

    @pl.loop(0, 2)
    def _(q):
        hidden_strip(q * (HR - D1))

    bias2 = jnp.broadcast_to(b2_ref[...], (SIDE, C))

    @pl.loop(0, D2 // N)
    def _(q):
        r = q * N
        for e, pre in rows_of(pair(hid, r + D2, N, D2, SIDE, D2, w2), D2):
            live = mask(r + e + VH, HH, SIDE)
            x = xm[r + e + VH, HH : HH + SIDE, :].astype(F32)
            out_ref[r + e] = (x + jnp.where(live, pre + bias2, 0.0)).astype(BF16)

    red2.finish(kg_ref.at[pl.ds(KR, KR)], kg_ref.at[pl.ds(2 * KR + 8, 1)])
    red1.finish(kg_ref.at[pl.ds(0, KR)], kg_ref.at[pl.ds(2 * KR, 1)])

    for a in range(2):
        for name in plans[a]:
            sent(a, name)


def on_device(x, gr, bin_valid, k1, b1, k2, b2):
    vmem = pl.BlockSpec(memory_space=pltpu.VMEM)
    smem = pl.BlockSpec(memory_space=pltpu.SMEM)
    hbm = pl.BlockSpec(memory_space=pl.ANY)
    block_out, feature_grad, kg = pl.pallas_call(
        main_kernel,
        out_shape=(
            jax.ShapeDtypeStruct((ROWS, SIDE, C), BF16),
            jax.ShapeDtypeStruct((ROWS, SIDE, C), BF16),
            jax.ShapeDtypeStruct((2 * KR + 16, C), F32),
        ),
        in_specs=[hbm, hbm, smem, vmem, vmem, vmem, vmem],
        out_specs=(vmem,) * 3,
        scratch_shapes=[
            pltpu.VMEM((PR, PC, C), BF16),
            pltpu.VMEM((PR, PC, C), BF16),
            pltpu.VMEM((PR, PC, C), BF16),
            pltpu.VMEM((PR, PC, C), BF16),
            pltpu.VMEM((HR, HC, C), BF16),
            pltpu.VMEM((HR, GC, C), F32),
            pltpu.VMEM((GR, GC, C), BF16),
            pltpu.VMEM((9 * C, C), BF16),
            pltpu.VMEM((9 * C, C), BF16),
            pltpu.VMEM((12 * C, 2 * C), BF16),
            pltpu.VMEM((12 * C, 2 * C), BF16),
            pltpu.VMEM((12 * C, 2 * C), BF16),
            pltpu.VMEM((12 * C, 2 * C), BF16),
            pltpu.VMEM((PC, C), jnp.int32),
            pltpu.VMEM((C, KR), F32),
            pltpu.VMEM((8, C), F32),
            pltpu.VMEM((2, 8, 4, PIECE, C), BF16),
            pltpu.VMEM((2, 7, 4, PIECE, C), BF16),
            pltpu.VMEM((2, 4, PIECE, C), F32),
            pltpu.VMEM((2, 4, PIECE, C), BF16),
            pltpu.VMEM((2, 3, PIECE, C), BF16),
            pltpu.VMEM((2, PIECE, C), BF16),
            pltpu.VMEM((2, 8, PIECE, C), BF16),
            pltpu.VMEM((2, 8, 4, PIECE, C), BF16),
            pltpu.SemaphoreType.DMA((2 * HALO,)),
            pltpu.SemaphoreType.DMA((2 * HALO,)),
            pltpu.SemaphoreType.DMA((2,)),
            pltpu.SemaphoreType.DMA((2 * COPIES,)),
            pltpu.SemaphoreType.DMA((2 * COPIES,)),
        ],
        compiler_params=pltpu.CompilerParams(
            collective_id=0, has_side_effects=True, vmem_limit_bytes=60 * 1024 * 1024
        ),
        name="resblock",
    )(x[0], gr[0], bin_valid, k1.reshape(9, C, C), b1[None], k2.reshape(9, C, C), b2[None])
    return (
        block_out[None],
        feature_grad[None],
        kg[:KR].reshape(3, 3, C, C),
        kg[2 * KR],
        kg[KR : 2 * KR].reshape(3, 3, C, C),
        kg[2 * KR + 8],
    )


def solution(mesh):
    strip = P("tile", "sub", None, None)
    return jax.shard_map(
        on_device,
        mesh=mesh,
        in_specs=(strip, strip, P(), P(), P(), P(), P()),
        out_specs=(strip, strip, P(), P(), P(), P()),
        check_vma=False,
    )
```
